32 devices in a mesh: vocab: 8 (over z, x), dp: 4 (over y, core).
Axes of the slice: x: 2, y: 2, z: 4, core: 2. Of those that a mesh axis runs over, the one named last changes fastest.
Arguments:
- teacher_hidden: bfloat16 [512, 5376], P('dp'), may hold values from -48 to 48
- student_hidden: bfloat16 [512, 2560], P('dp'), may hold values from -48 to 48
- teacher_codes: bfloat16 [16384, 5376], P(('vocab', 'dp')), may hold values from -8 to 7, as said below
- teacher_scales: float32 [16384, 42], P(('vocab', 'dp')), may hold values from 0.003 to 0.07
- student_weight: bfloat16 [16384, 2560], P(('vocab', 'dp')), may hold values from -1 to 1
- loss_scale: bfloat16 [512], P('dp'), may hold values from 2 to 20
Outputs:
- kl: float32 [512], P('dp')
- grad_hidden: bfloat16 [512, 2560], P('dp', 'vocab')
- grad_weight: bfloat16 [16384, 2560], P(('vocab', 'dp'))
The draws below stay inside these ranges and needn't reach their ends.
Inputs may be any that keep to these rules, and one draw needn't show every extreme that they name: `teacher_codes`: whole numbers.
All inputs are finite; a program needn't handle non-finite values.
Results may differ from the reference program's by a relative error of at most 0.0085.
Values may be sent and summed in bfloat16 or wider, within the bound.
A program may use at most 128 MiB of HBM per device.

```python
import math
import jax
import jax.numpy as jnp
from jax import lax

DT = 5376
DS = 2560
GROUP = 128
V_DEV = 512
TOKENS = 512
VOCAB = 16384
N_VOCAB = 8
N_DP = 4


def code_rows(key, row_ids):
    base_key = jax.random.fold_in(key, 101)

    def single(row_id):
        return jax.random.randint(jax.random.fold_in(base_key, row_id), (DT,), -8, 8).astype(jnp.float32)
    return jax.vmap(single)(row_ids)


def scale_rows(key, row_ids):
    base_key = jax.random.fold_in(key, 202)
    level_low, level_high, rise_total = (0.0085, 0.0105, 1.1)

    def single(row_id):
        key_pair = jax.random.split(jax.random.fold_in(base_key, row_id))
        scale_level = jnp.exp(jax.random.uniform(key_pair[0], (), jnp.float32, math.log(level_low), math.log(level_high)))
        jitter_factor = jnp.exp(jax.random.uniform(key_pair[1], (DT // GROUP,), jnp.float32, math.log(0.8), math.log(1.25)))
        rising_factor = jnp.exp(math.log(rise_total) * row_id.astype(jnp.float32) / VOCAB)
        return scale_level * rising_factor * jitter_factor
    return jax.vmap(single)(row_ids)


def student_rows(key, row_ids):
    base_key = jax.random.fold_in(key, 303)
    level_low, level_high, rise_total = (0.9, 1.2, 1.5)

    def single(row_id):
        key_pair = jax.random.split(jax.random.fold_in(base_key, row_id))
        scale_level = jnp.exp(jax.random.uniform(key_pair[0], (), jnp.float32, math.log(level_low), math.log(level_high)))
        rising_factor = jnp.exp(math.log(rise_total) * row_id.astype(jnp.float32) / VOCAB)
        values = jnp.clip(jax.random.normal(key_pair[1], (DS,), jnp.float32), -4.0, 4.0)
        return jnp.clip(scale_level * rising_factor * values / math.sqrt(DS), -1.0, 1.0)
    return jax.vmap(single)(row_ids).astype(jnp.bfloat16).astype(jnp.float32)


def hidden_draw(key, col_count, salt_value):
    key_list = jax.random.split(jax.random.fold_in(key, salt_value), 2)
    row_scale = jnp.exp(jax.random.uniform(key_list[0], (TOKENS, 1), jnp.float32, math.log(0.9), math.log(1.1)))
    values = jax.random.normal(key_list[1], (TOKENS, col_count), jnp.float32) * row_scale
    return jnp.clip(values, -48.0, 48.0).astype(jnp.bfloat16)


def draw_teacher_hidden(key, part):
    return hidden_draw(key, DT, 505)


def draw_student_hidden(key, part):
    return hidden_draw(key, DS, 606)


def draw_teacher_codes(key, part):
    return code_rows(key, jnp.arange(VOCAB, dtype=jnp.int32)).astype(jnp.bfloat16)


def draw_teacher_scales(key, part):
    return scale_rows(key, jnp.arange(VOCAB, dtype=jnp.int32)).astype(jnp.float32)


def draw_student_weight(key, part):
    return student_rows(key, jnp.arange(VOCAB, dtype=jnp.int32)).astype(jnp.bfloat16)


def steps_of(key, dims, pieces, least, largest):
    gain = 1.0
    for dim, blocks in pieces:
        steps = jax.random.uniform(jax.random.fold_in(jax.random.fold_in(key, 6), dim), (blocks,), jnp.float32, least / len(pieces), largest / len(pieces))
        gain = gain * jnp.repeat(jnp.exp(steps), dims[dim] // blocks).reshape((-1,) + (1,) * (len(dims) - 1 - dim))
    return gain


def setup_inputs(seed: int = 0) -> dict:
    seeds = jax.random.split(jax.random.key(seed), 7)
    return {
        "teacher_hidden": draw_teacher_hidden(jax.random.fold_in(seeds[6], 71), 0),
        "student_hidden": draw_student_hidden(jax.random.fold_in(seeds[6], 71), 0),
        "teacher_codes": draw_teacher_codes(jax.random.fold_in(seeds[6], 71), 0),
        "teacher_scales": draw_teacher_scales(jax.random.fold_in(seeds[6], 71), 0),
        "student_weight": draw_student_weight(jax.random.fold_in(seeds[6], 71), 0),
        "loss_scale": jnp.clip(jnp.exp(math.log(20.0) - 2.3025851 * jax.random.uniform(seeds[5], (TOKENS,), jnp.float32) ** steps_of(seeds[5], (TOKENS,), ((0, 4),), -0.2, 0.2)), 2.0, 20.0).astype(jnp.bfloat16),
    }


def dequantize(code_values, scales):
    row_count = code_values.shape[0]
    grouped = code_values.astype(jnp.float32).reshape(row_count, -1, GROUP) * scales.astype(jnp.float32)[:, :, None]
    return grouped.reshape(row_count, -1).astype(jnp.bfloat16)


def reference(teacher_hidden, student_hidden, teacher_codes, teacher_scales, student_weight, loss_scale):
    blocks = N_VOCAB * N_DP
    teacher_wide = teacher_hidden.astype(jnp.float32)
    student_wide = student_hidden.astype(jnp.float32)
    code_blocks = teacher_codes.reshape(blocks, V_DEV, DT)
    scale_blocks = teacher_scales.reshape(blocks, V_DEV, DT // GROUP)
    weight_blocks = student_weight.reshape(blocks, V_DEV, DS)

    def block_logits(members):
        code_values, scales, weight = members
        dequant_rows = dequantize(code_values, scales).astype(jnp.float32)
        teacher_part = jnp.dot(teacher_wide, dequant_rows.T, preferred_element_type=jnp.float32, precision=lax.Precision.HIGHEST)
        student_part = jnp.dot(student_wide, weight.astype(jnp.float32).T, preferred_element_type=jnp.float32, precision=lax.Precision.HIGHEST)
        return teacher_part, student_part

    teacher_logits, student_logits = lax.map(block_logits, (code_blocks, scale_blocks, weight_blocks))
    teacher_top = jnp.max(teacher_logits, axis=(0, 2))
    student_top = jnp.max(student_logits, axis=(0, 2))
    teacher_exp = jnp.exp(teacher_logits - teacher_top[None, :, None])
    teacher_total = jnp.sum(teacher_exp, axis=(0, 2))
    cross_total = jnp.sum(teacher_exp * (teacher_logits - student_logits), axis=(0, 2))
    student_total = jnp.sum(jnp.exp(student_logits - student_top[None, :, None]), axis=(0, 2))
    teacher_lse = teacher_top + jnp.log(teacher_total)
    student_lse = student_top + jnp.log(student_total)
    kl = cross_total / teacher_total - teacher_lse + student_lse
    teacher_prob = jnp.exp(teacher_logits - teacher_lse[None, :, None])
    student_prob = jnp.exp(student_logits - student_lse[None, :, None])
    logit_grad = (loss_scale.astype(jnp.float32)[None, :, None] * (student_prob - teacher_prob)).astype(jnp.bfloat16)

    def add_block(running, members):
        grad_block, weight = members
        product = jnp.dot(grad_block.astype(jnp.float32), weight.astype(jnp.float32), preferred_element_type=jnp.float32, precision=lax.Precision.HIGHEST)
        return running + product, None

    grad_hidden, unused = lax.scan(add_block, jnp.zeros((TOKENS, DS), jnp.float32), (logit_grad, weight_blocks))

    def weight_block(grad_block):
        product = jnp.dot(grad_block.astype(jnp.float32).T, student_wide, preferred_element_type=jnp.float32, precision=lax.Precision.HIGHEST)
        return product.astype(jnp.bfloat16)

    grad_weight = lax.map(weight_block, logit_grad).reshape(blocks * V_DEV, DS)
    return kl, grad_hidden.astype(jnp.bfloat16), grad_weight
```

```python
import functools

import jax
import jax.numpy as jnp
from jax import lax
from jax.experimental import pallas as pl
from jax.experimental.pallas import tpu as pltpu
from jax.sharding import PartitionSpec as P

GROUP = 128
LANE = 128
MESH = pl.DeviceIdType.MESH

PLAY_A = (
    "s1", "s2", "s3", "s4", "s5", "p0", "q0", "p1", "q1", "p2",
)
PLAY_B = (
    "y0", "q2", "y1", "p3", "y2", "x0", "q3", "y3", "x1", "y4", "f0", "00", "y5", "x2", "p4",
    "p5", "x3", "f1", "01", "x4", "f2", "02", "x5", "f3", "03", "f4", "04", "f5", "05",
)
PLAY_C = (
    "d0", "m0", "10", "d1", "m1", "11",
)
PLAY_D = (
    "p0", "q0", "p1", "q1", "p2", "q2", "p3", "q3", "d0", "d1", "s0", "p4", "d2", "s1", "p5",
)
PLAY_E = (
    "d3", "s2", "s3", "s4", "s5",
)
PLAY_F = (
    "m0", "00", "y0", "y1", "m1", "01", "y2", "x0", "m2", "02", "y3", "x1", "m3", "03", "y4",
    "f0", "m4", "04", "y5", "x2", "m5", "05",
)
PLAY_G = (
    "f1", "x3", "10", "f2", "11", "x4",
)
PLAY_H = (
    "f3", "12", "x5", "f4", "13", "f5",
)


def dot_t(left_rows, right_rows):
    return lax.dot_general(
        left_rows, right_rows, (((1,), (1,)), ((), ())), preferred_element_type=jnp.float32
    )


def chunk_widths(cols, lead):
    units = cols // 256
    head = [3] if lead and units > 3 else []
    rest = units - sum(head)
    per = max(k for k in (1, 2, 3, 5, 6, 7) if rest % k == 0)
    return [256 * n for n in head + [per] * (rest // per)]


def kernel(
    n_vocab, n_dp,
    th_own, sh_own, codes, scales, weight, loss_in,
    kl_out, gh_out, gw_out,
    th, sh, table, wgt, wgt_t, tlog, slog, lsc, stat, stat_b, fin, in_a, in_b,
    grad, gw_buf, mine, theirs, core_in,
    y1s, y1r, x1s, x1r, x2s, x2r, y2s, y2r, zs, zr, zf,
    sc_rows, loss_row, ld_sem, gw_sem, pc_s, pc_r, hop_s, hop_r,
    ls_s, ls_r, a_s, a_r, b_s, b_r, cs, cr, r1s, r1r, r2s, r2r, z_ss, z_rs,
):
    v, d = lax.axis_index("vocab"), lax.axis_index("dp")
    core, y = lax.rem(d, 2), lax.div(d, 2)
    p, q = lax.rem(v, 2), lax.div(v, 2)
    n_y, n_z = n_dp // 2, n_vocab // 2
    v_pair = 2 * q + 1 - p
    r = lax.rem(q, 2)
    v_quad = 2 * (q + 1 - 2 * r) + p
    tok = th_own.shape[0]
    rv = zr.shape[1]
    n_z1 = n_z // 2
    span = n_y * tok
    quarter = tok // 4

    def rcopy(src, dst, send, recv, dev):
        return pltpu.make_async_remote_copy(
            src_ref=src, dst_ref=dst, send_sem=send, recv_sem=recv,
            device_id=dev, device_id_type=MESH,
        )

    peers_a = []
    for dv in range(2):
        for dd in range(n_dp):
            if dv or dd:
                peers_a.append((v if dv == 0 else v_pair, lax.rem(d + dd, n_dp)))
    peers_b = [(2 * lax.rem(q + o, n_z) + p, d) for o in range(1, n_z)]
    barrier = pltpu.get_barrier_semaphore()
    for peer in peers_a + peers_b:
        pl.semaphore_signal(barrier, inc=1, device_id=peer, device_id_type=MESH)

    chunks = []
    for own, scr, tab, acc in ((th_own, th, table, tlog), (sh_own, sh, wgt, slog)):
        base = 0
        for width in chunk_widths(own.shape[1], tab is table):
            chunks.append((own, scr, tab, acc, base, width))
            base += width
    n_ch = len(chunks)
    firsts = [k == 0 or chunks[k][3] is not chunks[k - 1][3] for k in range(n_ch)]
    by_y = [False] * n_ch
    room = sum(ch[5] for ch in chunks) * 55 // 100
    for k in reversed(range(n_ch)):
        room -= chunks[k][5]
        if room < 0:
            break
        by_y[k] = True

    def block(g, yy):
        return pl.multiple_of((g * n_y + yy) * tok, tok)

    my_rows = pl.ds(pl.multiple_of((core * n_y + y) * tok, tok), tok)
    loads = []
    for k, (own, scr, tab, acc, base, width) in enumerate(chunks):
        src = codes if tab is table else weight
        cp = pltpu.make_async_copy(
            src.at[:, pl.ds(base, width)], tab.at[:, pl.ds(base, width)], ld_sem.at[k]
        )
        cp.start()
        loads.append(cp)
    own_loads = [
        pltpu.make_async_copy(th_own, th.at[my_rows], ld_sem.at[n_ch]),
        pltpu.make_async_copy(sh_own, sh.at[my_rows], ld_sem.at[n_ch + 1]),
    ]
    for cp in own_loads:
        cp.start()
    groups = scales.shape[0]
    pad = jnp.zeros((sc_rows.shape[1] - groups, LANE), jnp.float32)
    for b in range(0, scales.shape[1], LANE):
        sc_rows[pl.ds(b, LANE), :] = jnp.concatenate(
            [scales[:, pl.ds(b, LANE)], pad], axis=0
        ).T
    loss_row[...] = jnp.broadcast_to(
        loss_in[...].astype(jnp.float32).reshape(1, tok), loss_row.shape
    )
    lsc[core * n_y + y] = loss_row[...]
    with jax.named_scope("barrier"):
        pl.semaphore_wait(barrier, len(peers_a) + len(peers_b))

    A, B, C, E = 2 * r + p, 2 * r + 1 - p, 2 * (1 - r) + p, 2 * (1 - r) + 1 - p
    Y_A, Y_E, X_A, Z_A, X_C, Z_B, D_A, D_B, D_C, D_E = range(10)
    order = []
    for i in range(n_z1):
        order += [i, n_z1 + i]
    order += [i for i in range(n_z) if i not in order]
    n_gw = sh.shape[1] // 512

    def run(c):
        mate = 2 * y + 1 - c
        X, Z = (v_pair, d), (v_quad, d)
        sends = []
        gw_copies = []

        def launch(cp):
            cp.start()
            sends.append(cp)

        def region(g, k, yy, piece, half=None):
            scr, base, width = chunks[k][1], chunks[k][4], chunks[k][5]
            first, size = block(g, yy) + piece * quarter, quarter
            if half is not None:
                size = quarter // 2
                first += half * size
            return scr.at[pl.ds(pl.multiple_of(first, size), size), pl.ds(base, width)]

        def came(o):
            return lax.rem(y + n_y - o, n_y)

        def y_send(k, kind):
            own, base, width = chunks[k][0], chunks[k][4], chunks[k][5]
            piece = A if kind == Y_A else E
            src = own.at[
                pl.ds(pl.multiple_of(piece * quarter, quarter), quarter), pl.ds(base, width)
            ]
            for o in range(1, n_y):
                to = 2 * lax.rem(y + o, n_y) + c
                launch(rcopy(
                    src, region(c, k, y, piece),
                    hop_s.at[kind, o - 1, k], hop_r.at[kind, o - 1, k], (v, to),
                ))

        def hop(kind, k, o, g, piece, dev, half=None):
            ref = region(g, k, came(o), piece, half)
            return rcopy(ref, ref, hop_s.at[kind, o - 1, k], hop_r.at[kind, o - 1, k], dev)

        def to_mate(kind, k, o, piece):
            launch(hop(kind, k, o, c, piece, (v, mate)))

        def stage_y(k):
            for o in range(1, n_y):
                hop(Y_A, k, o, c, A, X).wait_recv()
                launch(hop(X_A, k, o, c, A, X))
                launch(hop(Z_A, k, o, c, A, Z))
                to_mate(D_A, k, o, A)

        def stage_xz(k):
            for o in range(1, n_y):
                hop(X_A, k, o, c, B, X).wait_recv()
                if not by_y[k]:
                    launch(hop(Z_B, k, o, c, B, Z, 1))
                to_mate(D_B, k, o, B)
                hop(Z_A, k, o, c, C, Z).wait_recv()
                if not by_y[k]:
                    launch(hop(X_C, k, o, c, C, X, 0))
                to_mate(D_C, k, o, C)

        def stage_far(k):
            for o in range(1, n_y):
                if by_y[k]:
                    hop(Y_E, k, o, c, E, X).wait_recv()
                else:
                    hop(X_C, k, o, c, E, X, 0).wait_recv()
                    hop(Z_B, k, o, c, E, Z, 1).wait_recv()
                to_mate(D_E, k, o, E)

        def mate_wait(k, pairs):
            for o in range(1, n_y):
                for kind, piece in pairs:
                    hop(kind, k, o, 1 - c, piece, X).wait_recv()

        first_pair = [(D_A, A)]
        rest_pairs = [(D_B, B), (D_C, C), (D_E, E)]

        def prepare(k, half):
            own, scr, tab, acc, base, width = chunks[k]
            if half == 0:
                loads[k].wait()
            steps = table.shape[0] // 128
            if tab is table:
                @pl.loop(half * steps, (half + 1) * steps)
                def _(i):
                    rsl = pl.ds(pl.multiple_of(i * 64, 64), 64)
                    sc = sc_rows[rsl, :]
                    for g in range(width // GROUP):
                        lane = pl.ds(base + g * GROUP, GROUP)
                        col = (base + g * GROUP) // GROUP
                        wide = table[rsl, lane].astype(jnp.float32) * sc[:, col : col + 1]
                        table[rsl, lane] = wide.astype(jnp.bfloat16)
            elif half == 0:
                for b in range(base, base + width, 256):
                    wgt_t[pl.ds(b, 256), :] = wgt[:, pl.ds(b, 256)].T

        def product(g, k):
            own, scr, tab, acc, base, width = chunks[k]
            for b in range(g * span, (g + 1) * span, 2 * tok):
                two = pl.ds(b, 2 * tok)
                part = dot_t(tab[:, pl.ds(base, width)], scr[two, pl.ds(base, width)])
                if firsts[k]:
                    acc[:, two] = part
                else:
                    acc[:, two] += part

        def local_stat(g):
            @pl.loop(0, n_y)
            def _(j):
                off = pl.multiple_of(j * tok, tok)
                sl = pl.ds(pl.multiple_of(g * span + j * tok, tok), tok)
                t_max = jnp.max(tlog[:, sl], axis=0, keepdims=True)
                s_max = jnp.max(slog[:, sl], axis=0, keepdims=True)
                te = jnp.exp(tlog[:, sl] - t_max)
                t_sum = jnp.sum(te, axis=0, keepdims=True)
                x_sum = jnp.sum(te * (tlog[:, sl] - slog[:, sl]), axis=0, keepdims=True)
                tlog[:, sl] = te
                se = jnp.exp(slog[:, sl] - s_max)
                s_sum = jnp.sum(se, axis=0, keepdims=True)
                slog[:, sl] = se
                stat[g, :, pl.ds(off, tok)] = jnp.concatenate(
                    [t_max, t_sum, x_sum, s_max, s_sum, jnp.zeros((3, tok), jnp.float32)],
                    axis=0,
                )

        def merge(parts):
            t_top = functools.reduce(jnp.maximum, [x[0:1] for x in parts])
            s_top = functools.reduce(jnp.maximum, [x[3:4] for x in parts])
            t_sum = x_sum = s_sum = 0.0
            for x in parts:
                t_w = jnp.exp(x[0:1] - t_top)
                t_sum += x[1:2] * t_w
                x_sum += x[2:3] * t_w
                s_sum += x[4:5] * jnp.exp(x[3:4] - s_top)
            return t_top, t_sum, x_sum, s_top, s_sum

        def a_copy(g, i):
            return rcopy(stat.at[g], in_a.at[g, i], a_s.at[g, i], a_r.at[g, i], peers_a[i])

        def b_copy(g, i):
            return rcopy(stat_b.at[g], in_b.at[g, i], b_s.at[g, i], b_r.at[g, i], peers_b[i])

        def send_a(g):
            local_stat(g)
            for i in reversed(range(len(peers_a))):
                launch(a_copy(g, i))

        def send_b(g):
            for i in range(len(peers_a)):
                a_copy(g, i).wait_recv()
            stat_b[g] = jnp.concatenate(
                list(merge([stat[g]] + [in_a[g, i] for i in range(len(peers_a))]))
                + [jnp.zeros((3, span), jnp.float32)], axis=0
            )
            for i in range(len(peers_b)):
                launch(b_copy(g, i))

        def finish(g):
            for i in range(len(peers_b)):
                b_copy(g, i).wait_recv()
            t_top, t_sum, x_sum, s_top, s_sum = merge(
                [stat_b[g]] + [in_b[g, i] for i in range(len(peers_b))]
            )
            t_lse = t_top + jnp.log(t_sum)
            s_lse = s_top + jnp.log(s_sum)
            fin[g] = jnp.concatenate(
                [
                    x_sum / t_sum - t_lse + s_lse,
                    jnp.exp(stat[g, 0:1] - t_lse),
                    jnp.exp(stat[g, 3:4] - s_lse),
                    jnp.zeros((5, span), jnp.float32),
                ],
                axis=0,
            )
            if g == c:
                kl_out[...] = fin[g, 0:1, pl.ds(pl.multiple_of(y * tok, tok), tok)]

            @pl.loop(0, n_y)
            def _(j):
                off = pl.multiple_of(j * tok, tok)
                sl = pl.ds(pl.multiple_of(g * span + j * tok, tok), tok)
                f = fin[g, :, pl.ds(off, tok)]
                grad[:, sl] = (
                    lsc[g * n_y + j][0:1] * (slog[:, sl] * f[2:3] - tlog[:, sl] * f[1:2])
                ).astype(jnp.bfloat16)

        def hidden(g, z):
            for pp in range(2):
                feat = wgt_t[pl.ds((2 * z + pp) * rv, rv), :]
                for yy in range(0, n_y, 2):
                    part = jnp.dot(
                        feat, grad[:, pl.ds(g * span + yy * tok, 2 * tok)],
                        preferred_element_type=jnp.float32,
                    )
                    for h in range(2):
                        one = part[:, h * tok : (h + 1) * tok]
                        if g == c:
                            mine[z, pp, yy + h] = one
                        else:
                            theirs[z, pp, yy + h] = one.astype(jnp.bfloat16)
            if g != c:
                launch(core_copy(z))

        def core_copy(z):
            return rcopy(theirs.at[z], core_in.at[z], cs.at[z], cr.at[z], (v, mate))

        def y1_copy(z, o):
            to = 2 * lax.rem(y + o, n_y) + c
            return rcopy(
                y1s.at[z, o - 1], y1r.at[z, o - 1], r1s.at[z, o - 1], r1r.at[z, o - 1], (v, to)
            )

        def x1_copy(z):
            return rcopy(x1s.at[z], x1r.at[z], r2s.at[z, 0], r2r.at[z, 0], (v_pair, d))

        def x2_copy(z):
            return rcopy(
                x2s.at[z - n_z1], x2r.at[z - n_z1], r1s.at[z, 0], r1r.at[z, 0], (v_pair, d)
            )

        def y2_copy(z, o):
            to = 2 * lax.rem(y + o, n_y) + c
            return rcopy(
                y2s.at[z - n_z1, o - 1], y2r.at[z - n_z1, o - 1],
                r2s.at[z, o - 1], r2r.at[z, o - 1], (v, to),
            )

        def after_core(z):
            core_copy(z).wait_recv()
            if z < n_z1:
                for o in range(1, n_y):
                    to = lax.rem(y + o, n_y)
                    for pp in range(2):
                        y1s[z, o - 1, pp] = (
                            mine[z, pp, to] + core_in[z, pp, to].astype(jnp.float32)
                        ).astype(jnp.bfloat16)
                    launch(y1_copy(z, o))
            else:
                for yy in range(n_y):
                    x2s[z - n_z1, yy] = (
                        mine[z, 1 - p, yy] + core_in[z, 1 - p, yy].astype(jnp.float32)
                    ).astype(jnp.bfloat16)
                launch(x2_copy(z))

        def after_first(z):
            if z < n_z1:
                for o in range(1, n_y):
                    y1_copy(z, o).wait_recv()

                def total(which):
                    out = mine[z, which, y] + core_in[z, which, y].astype(jnp.float32)
                    for o in range(1, n_y):
                        out += y1r[z, o - 1, which].astype(jnp.float32)
                    return out

                x1s[z] = total(1 - p).astype(jnp.bfloat16)
                launch(x1_copy(z))
                zf[z] = total(p)
            else:
                x2_copy(z).wait_recv()

                def total(yy):
                    return (
                        mine[z, p, yy] + core_in[z, p, yy].astype(jnp.float32)
                        + x2r[z - n_z1, yy].astype(jnp.float32)
                    )

                for o in range(1, n_y):
                    y2s[z - n_z1, o - 1] = total(lax.rem(y + o, n_y)).astype(jnp.bfloat16)
                    launch(y2_copy(z, o))
                zf[z] = total(y)

        def z_copy(z):
            return rcopy(zs.at[z], zr.at[q], z_ss.at[z], z_rs.at[q], (2 * z + p, d))

        def after_second(z):
            if z < n_z1:
                x1_copy(z).wait_recv()
                full = zf[z] + x1r[z].astype(jnp.float32)
            else:
                full = zf[z]
                for o in range(1, n_y):
                    y2_copy(z, o).wait_recv()
                    full += y2r[z - n_z1, o - 1].astype(jnp.float32)
            zf[z] = full
            zs[z] = full.astype(jnp.bfloat16)

            @pl.when(q != z)
            def _():
                z_copy(z).start()

        def weight_part(b):
            sl = pl.ds(b * 512, 512)
            gw_buf[:, sl] = jnp.dot(
                grad[...], sh[:, sl], preferred_element_type=jnp.float32
            ).astype(jnp.bfloat16)
            cp = pltpu.make_async_copy(gw_buf.at[:, sl], gw_out.at[:, sl], gw_sem.at[b])
            cp.start()
            gw_copies.append(cp)

        def last():
            total = zf[q]
            for o in range(1, n_z):
                src = lax.rem(q + o, n_z)
                rcopy(
                    zs.at[src], zr.at[src], z_ss.at[src], z_rs.at[src], (v_pair, d)
                ).wait_recv()
                total += zr[src].astype(jnp.float32)
            gh_out[...] = total.astype(jnp.bfloat16)

        def loss_wait():
            for dd in range(1, n_dp):
                other = lax.rem(d + n_dp - dd, n_dp)
                slot = lax.rem(other, 2) * n_y + lax.div(other, 2)
                rcopy(
                    loss_row, lsc.at[slot], ls_s.at[dd - 1], ls_r.at[dd - 1], (v, mate)
                ).wait_recv()

        def mate_copies():
            for i, (own, scr) in enumerate(((th_own, th), (sh_own, sh))):
                launch(rcopy(
                    own, scr.at[pl.ds(block(c, y), tok)], pc_s.at[i], pc_r.at[i], (v, mate)
                ))

        def mate_arrived():
            for i, (own, scr) in enumerate(((th_own, th), (sh_own, sh))):
                rcopy(
                    own, scr.at[pl.ds(block(1 - c, y), tok)], pc_s.at[i], pc_r.at[i], (v, mate)
                ).wait_recv()

        def named(name, fn, *args):
            with jax.named_scope(name + "_".join(str(x) for x in args if isinstance(x, int))):
                fn(*args)

        for dd in range(1, n_dp):
            launch(rcopy(
                loss_row, lsc.at[c * n_y + y], ls_s.at[dd - 1], ls_r.at[dd - 1],
                (v, lax.rem(d + dd, n_dp)),
            ))
        far = [k for k in range(n_ch) if by_y[k]]

        def send_y(k):
            y_send(k, Y_A)
            if k == n_ch - 1:
                for kk in far:
                    y_send(kk, Y_E)

        ops = {
            "p": lambda k: prepare(k, 0),
            "q": lambda k: prepare(k, 1),
            "s": send_y,
            "y": stage_y,
            "x": stage_xz,
            "f": stage_far,
            "d": lambda k: mate_wait(k, first_pair),
            "m": lambda k: mate_wait(k, rest_pairs),
            "0": lambda k: product(0, k),
            "1": lambda k: product(1, k),
        }
        done = set()

        def play(steps, flush):
            todo = [(step[0], int(step[1:])) for step in steps]
            todo += [(name, k) for k in range(n_ch) for name in flush]
            for name, k in todo:
                if k < n_ch and (name, k) not in done:
                    done.add((name, k))
                    named(name, ops[name], k)

        if c == 0:
            play(("s0",), "")
            mate_copies()
            play(PLAY_A, "")
            for cp in own_loads:
                cp.wait()
            play(PLAY_B, "spqyxf0")
            named("send_a", send_a, 0)
            named("mate_arrived", mate_arrived)
            play(PLAY_C, "")
            named("send_b", send_b, 0)
            play((), "dm1")
            named("send_a", send_a, 1)
            loss_wait()
            named("finish", finish, 0)
            for i, z in enumerate(order):
                named("hidden", hidden, 0, z)
                if i >= 1:
                    named("after_core", after_core, order[i - 1])
            named("after_core", after_core, order[-1])
            named("send_b", send_b, 1)
            named("finish", finish, 1)
            for z in order:
                named("hidden", hidden, 1, z)
            for z in order:
                named("after_first", after_first, z)
            for b in range(n_gw):
                named("weight", weight_part, b)
            for z in order:
                named("after_second", after_second, z)
            named("last", last)
        else:
            mate_copies()
            play(PLAY_D, "pq")
            for cp in own_loads:
                cp.wait()
            play(PLAY_E, "ds")
            named("mate_arrived", mate_arrived)
            play(PLAY_F, "m0")
            named("send_a", send_a, 0)
            play(PLAY_G, "")
            named("send_b", send_b, 0)
            play(PLAY_H, "yxf1")
            named("send_a", send_a, 1)
            loss_wait()
            named("finish", finish, 0)
            for z in order:
                named("hidden", hidden, 0, z)
            named("send_b", send_b, 1)
            named("finish", finish, 1)
            for i, z in enumerate(order):
                named("hidden", hidden, 1, z)
                if i >= 1:
                    named("after_core", after_core, order[i - 1])
            named("after_core", after_core, order[-1])
            for b in range(n_gw):
                named("weight", weight_part, b)
            for z in order:
                named("after_first", after_first, z)
            for z in order:
                named("after_second", after_second, z)
            named("last", last)

        for cp in sends:
            cp.wait_send()
        for o in range(1, n_z):
            dst = lax.rem(q + o, n_z)
            rcopy(zs.at[dst], zr.at[q], z_ss.at[dst], z_rs.at[q], (2 * dst + p, d)).wait_send()
        for cp in gw_copies:
            cp.wait()

    for which in range(2):
        pl.when(core == which)(functools.partial(run, which))


def hand_over(kl, gh, gw):
    parts = 4
    step = gw.shape[0] // parts

    def move(kl_in, gh_in, gw_in, kl_to, gh_to, gw_to, kl_v, gh_v, gw_v, sem_in, sem_out):
        plan = [(kl_in, kl_v, kl_to), (gh_in, gh_v, gh_to)]
        for i in range(parts):
            sl = pl.ds(i * step, step)
            plan.append((gw_in.at[sl], gw_v.at[sl], gw_to.at[sl]))
        reads = [pltpu.make_async_copy(a, b, sem_in.at[i]) for i, (a, b, _) in enumerate(plan)]
        writes = [pltpu.make_async_copy(b, e, sem_out.at[i]) for i, (_, b, e) in enumerate(plan)]
        for cp in reads:
            cp.start()
        for cp, out in zip(reads, writes):
            cp.wait()
            out.start()
        for out in writes:
            out.wait()

    spec = pl.BlockSpec(memory_space=pl.ANY)
    arrays = (kl, gh, gw)
    return pl.pallas_call(
        move,
        out_shape=tuple(jax.ShapeDtypeStruct(a.shape, a.dtype) for a in arrays),
        in_specs=[spec] * 3,
        out_specs=(spec,) * 3,
        scratch_shapes=[pltpu.VMEM(a.shape, a.dtype) for a in arrays]
        + [pltpu.SemaphoreType.DMA((parts + 2,))] * 2,
        name="hand_over",
    )(*arrays)


def solution(mesh):
    n_vocab, n_dp = mesh.shape["vocab"], mesh.shape["dp"]

    def local(th_own, sh_own, codes, scales, weight, loss_scale):
        tok, dt = th_own.shape
        ds_ = sh_own.shape[1]
        rows = codes.shape[0]
        n_tok = tok * n_dp
        n_y, n_z = n_dp // 2, n_vocab // 2
        n_off, n_z1 = n_y - 1, n_z // 2
        n_z2 = n_z - n_z1
        rv = ds_ // n_vocab
        n_ch = len(chunk_widths(dt, True)) + len(chunk_widths(ds_, False))
        span = n_y * tok
        n_a, n_b = 2 * n_dp - 1, n_z - 1
        bf, f32 = jnp.bfloat16, jnp.float32
        V, D = pltpu.VMEM, pltpu.SemaphoreType.DMA
        any_spec = pl.BlockSpec(memory_space=pl.ANY)
        vm_spec = pl.BlockSpec(memory_space=pltpu.VMEM)
        kl, gh, gw = pl.pallas_call(
            functools.partial(kernel, n_vocab, n_dp),
            out_shape=(
                jax.ShapeDtypeStruct((1, tok), f32),
                jax.ShapeDtypeStruct((rv, tok), bf),
                jax.ShapeDtypeStruct((rows, ds_), bf),
            ),
            in_specs=[any_spec, any_spec, any_spec, vm_spec, any_spec, vm_spec],
            out_specs=(vm_spec, vm_spec, any_spec),
            scratch_shapes=[
                V((n_tok, dt), bf), V((n_tok, ds_), bf), V((rows, dt), bf), V((rows, ds_), bf),
                V((ds_, rows), bf), V((rows, n_tok), f32), V((rows, n_tok), f32),
                V((n_dp, 8, tok), f32), V((2, 8, span), f32), V((2, 8, span), f32),
                V((2, 8, span), f32), V((2, n_a, 8, span), f32), V((2, n_b, 8, span), f32),
                V((rows, n_tok), bf), V((rows, ds_), bf),
                V((n_z, 2, n_y, rv, tok), f32), V((n_z, 2, n_y, rv, tok), bf),
                V((n_z, 2, n_y, rv, tok), bf),
                V((n_z1, n_off, 2, rv, tok), bf), V((n_z1, n_off, 2, rv, tok), bf),
                V((n_z1, rv, tok), bf), V((n_z1, rv, tok), bf),
                V((n_z2, n_y, rv, tok), bf), V((n_z2, n_y, rv, tok), bf),
                V((n_z2, n_off, rv, tok), bf), V((n_z2, n_off, rv, tok), bf),
                V((n_z, rv, tok), bf), V((n_z, rv, tok), bf), V((n_z, rv, tok), f32),
                V((rows, -(-scales.shape[1] // 8) * 8), f32), V((8, tok), f32),
                D((n_ch + 2,)), D((ds_ // 512,)), D((2,)), D((2,)),
                D((10, n_off, n_ch)), D((10, n_off, n_ch)),
                D((n_dp - 1,)), D((n_dp - 1,)), *[D((2, n_a))] * 2, *[D((2, n_b))] * 2,
                D((n_z,)), D((n_z,)), *[D((n_z, n_off))] * 4, D((n_z,)), D((n_z,)),
            ],
            compiler_params=pltpu.CompilerParams(
                collective_id=0, has_side_effects=True, vmem_limit_bytes=60 * 1024 * 1024
            ),
            name="distill",
        )(th_own, sh_own, codes, scales.T, weight, loss_scale)
        kl, gh, gw = hand_over(kl, gh, gw)
        return kl.reshape(tok), gh.T, gw

    in_specs = (
        P("dp", None),
        P("dp", None),
        P(("vocab", "dp"), None),
        P(("vocab", "dp"), None),
        P(("vocab", "dp"), None),
        P("dp"),
    )
    out_specs = (P("dp"), P("dp", "vocab"), P(("vocab", "dp"), None))
    return jax.shard_map(local, mesh=mesh, in_specs=in_specs, out_specs=out_specs, check_vma=False)
```

```python
import functools

import jax
import jax.numpy as jnp
from jax import lax
from jax.experimental import pallas as pl
from jax.experimental.pallas import tpu as pltpu
from jax.sharding import PartitionSpec as P

GROUP = 128
LANE = 128
MESH = pl.DeviceIdType.MESH

PLAY_A = (
    "s1", "s2", "s3", "s4", "s5", "p0", "q0", "p1", "q1", "p2",
)
PLAY_B = (
    "y0", "q2", "y1", "p3", "y2", "q3", "y3", "x0", "y4", "x1", "y5", "p4", "p5", "x2", "f0",
    "00", "x3", "f1", "01", "x4", "f3", "03", "x5", "f4", "04", "f5", "05", "f2", "02",
)
PLAY_C = (
    "d0", "m0", "10", "d1", "m1", "11",
)
PLAY_I = (
    "d3", "m3", "13", "d4", "m4", "14", "d5", "m5", "15",
)
PLAY_D = (
    "p0", "q0", "p1", "q1", "p2", "q2", "p3", "q3", "d0", "s0", "d1", "s1", "p4", "d2", "s2",
    "p5",
)
PLAY_E = (
    "d3", "s3", "s4", "s5",
)
PLAY_F = (
    "y0", "y1", "m0", "00", "y2", "x0", "m1", "01", "y3", "x1", "m3", "03", "y4", "x2", "m4",
    "04", "y5", "f0", "m5", "05", "d5", "m2", "02",
)
PLAY_G = (
    "x3", "f1", "10", "x4", "11", "x5",
)
PLAY_H = (
    "f3", "13", "f4", "14", "f5", "15", "f2", "12",
)


def dot_t(left_rows, right_rows):
    return lax.dot_general(
        left_rows, right_rows, (((1,), (1,)), ((), ())), preferred_element_type=jnp.float32
    )


def chunk_widths(cols, lead):
    units = cols // 256
    head = [3] if lead and units > 3 else []
    rest = units - sum(head)
    per = max(k for k in (1, 2, 3, 5, 6, 7) if rest % k == 0)
    return [256 * n for n in head + [per] * (rest // per)]


def kernel(
    n_vocab, n_dp,
    th_own, sh_own, codes, scales, weight, loss_in,
    kl_out, gh_out, gw_out,
    th, sh, table, wgt, wgt_t, tlog, slog, lsc, stat, stat_b, fin, in_a, in_b,
    grad, mine, theirs, core_in,
    y1s, y1r, x1s, x1r, x2s, x2r, y2s, y2r, zs, zr, zf,
    sc_rows, loss_row, ld_sem, pc_r, hop_r, sent, ls_r, a_r, b_r, cr, r1r, r2r, z_rs,
):
    v, d = lax.axis_index("vocab"), lax.axis_index("dp")
    core, y = lax.rem(d, 2), lax.div(d, 2)
    p, q = lax.rem(v, 2), lax.div(v, 2)
    n_y, n_z = n_dp // 2, n_vocab // 2
    v_pair = 2 * q + 1 - p
    r = lax.rem(q, 2)
    v_quad = 2 * (q + 1 - 2 * r) + p
    tok = th_own.shape[0]
    rv = zr.shape[1]
    n_z1 = n_z // 2
    span = n_y * tok
    quarter = tok // 4

    def rcopy(src, dst, recv, dev):
        return pltpu.make_async_remote_copy(
            src_ref=src, dst_ref=dst, send_sem=sent, recv_sem=recv,
            device_id=dev, device_id_type=MESH,
        )

    peers_a = []
    for dv in range(2):
        for dd in range(n_dp):
            if dv or dd:
                peers_a.append((v if dv == 0 else v_pair, lax.rem(d + dd, n_dp)))
    peers_b = [(2 * lax.rem(q + o, n_z) + p, d) for o in range(1, n_z)]
    barrier = pltpu.get_barrier_semaphore()
    for peer in peers_a + peers_b:
        pl.semaphore_signal(barrier, inc=1, device_id=peer, device_id_type=MESH)

    chunks = []
    for own, scr, tab, acc in ((th_own, th, table, tlog), (sh_own, sh, wgt, slog)):
        base = 0
        for width in chunk_widths(own.shape[1], tab is table):
            chunks.append((own, scr, tab, acc, base, width))
            base += width
    n_ch = len(chunks)
    firsts = [k == 0 or chunks[k][3] is not chunks[k - 1][3] for k in range(n_ch)]
    by_y = [False] * n_ch
    room = sum(ch[5] for ch in chunks) * 55 // 100
    for k in reversed(range(n_ch)):
        room -= chunks[k][5]
        if room < 0:
            break
        by_y[k] = True

    def block(g, yy):
        return pl.multiple_of((g * n_y + yy) * tok, tok)

    my_rows = pl.ds(pl.multiple_of((core * n_y + y) * tok, tok), tok)
    loads = []
    for k, (own, scr, tab, acc, base, width) in enumerate(chunks):
        src = codes if tab is table else weight
        cp = pltpu.make_async_copy(
            src.at[:, pl.ds(base, width)], tab.at[:, pl.ds(base, width)], ld_sem.at[k]
        )
        cp.start()
        loads.append(cp)
    own_loads = [
        pltpu.make_async_copy(th_own, th.at[my_rows], ld_sem.at[n_ch]),
        pltpu.make_async_copy(sh_own, sh.at[my_rows], ld_sem.at[n_ch + 1]),
    ]
    for cp in own_loads:
        cp.start()
    groups = scales.shape[0]
    pad = jnp.zeros((sc_rows.shape[1] - groups, LANE), jnp.float32)
    for b in range(0, scales.shape[1], LANE):
        sc_rows[pl.ds(b, LANE), :] = jnp.concatenate(
            [scales[:, pl.ds(b, LANE)], pad], axis=0
        ).T
    loss_row[...] = jnp.broadcast_to(
        loss_in[...].astype(jnp.float32).reshape(1, tok), loss_row.shape
    )
    lsc[core * n_y + y] = loss_row[...]
    with jax.named_scope("barrier"):
        pl.semaphore_wait(barrier, len(peers_a) + len(peers_b))

    A, B, C, E = 2 * r + p, 2 * r + 1 - p, 2 * (1 - r) + p, 2 * (1 - r) + 1 - p
    Y_A, X_A, Z_A, FAR, D_A, D_REST = range(6)
    order = []
    for i in range(n_z1):
        order += [i, n_z1 + i]
    order += [i for i in range(n_z) if i not in order]
    n_gw = sh.shape[1] // 512

    def run(c):
        mate = 2 * y + 1 - c
        X, Z = (v_pair, d), (v_quad, d)
        sends = []

        def launch(cp):
            cp.start()
            sends.append(cp)

        def region(g, k, yy, piece, half=None):
            scr, base, width = chunks[k][1], chunks[k][4], chunks[k][5]
            first, size = block(g, yy) + piece * quarter, quarter
            if half is not None:
                size = quarter // 2
                first += half * size
            return scr.at[pl.ds(pl.multiple_of(first, size), size), pl.ds(base, width)]

        def came(o):
            return lax.rem(y + n_y - o, n_y)

        def y_send(k, kind):
            own, base, width = chunks[k][0], chunks[k][4], chunks[k][5]
            piece = A if kind == Y_A else E
            src = own.at[
                pl.ds(pl.multiple_of(piece * quarter, quarter), quarter), pl.ds(base, width)
            ]
            for o in range(1, n_y):
                to = 2 * lax.rem(y + o, n_y) + c
                launch(rcopy(src, region(c, k, y, piece), hop_r.at[kind, o - 1, k], (v, to)))

        def hop(kind, k, o, piece, dev, half=None):
            ref = region(c, k, came(o), piece, half)
            return rcopy(ref, ref, hop_r.at[kind, o - 1, k], dev)

        def to_mate(kind, k, o, piece):
            launch(hop(kind, k, o, piece, (v, mate)))

        def stage_y(k):
            for o in range(1, n_y):
                hop(Y_A, k, o, A, X).wait_recv()
                launch(hop(X_A, k, o, A, X))
                launch(hop(Z_A, k, o, A, Z))
                to_mate(D_A, k, o, A)

        def stage_xz(k):
            for o in range(1, n_y):
                hop(X_A, k, o, B, X).wait_recv()
                if not by_y[k]:
                    launch(hop(FAR, k, o, B, Z, 1))
                to_mate(D_REST, k, o, B)
                hop(Z_A, k, o, C, Z).wait_recv()
                if not by_y[k]:
                    launch(hop(FAR, k, o, C, X, 0))
                to_mate(D_REST, k, o, C)

        def stage_far(k):
            for o in range(1, n_y):
                hop(FAR, k, o, E, X).wait_recv()
                to_mate(D_REST, k, o, E)

        def mate_wait(kind, k):
            scr, base, width = chunks[k][1], chunks[k][4], chunks[k][5]
            size = quarter if kind == D_A else 3 * quarter
            for o in range(1, n_y):
                ref = scr.at[pl.ds(block(1 - c, came(o)), size), pl.ds(base, width)]
                rcopy(ref, ref, hop_r.at[kind, o - 1, k], X).wait_recv()

        def prepare(k, half):
            own, scr, tab, acc, base, width = chunks[k]
            if half == 0:
                loads[k].wait()
            steps = table.shape[0] // 128
            if tab is table:
                @pl.loop(half * steps, (half + 1) * steps)
                def _(i):
                    rsl = pl.ds(pl.multiple_of(i * 64, 64), 64)
                    sc = sc_rows[rsl, :]
                    for g in range(width // GROUP):
                        lane = pl.ds(base + g * GROUP, GROUP)
                        col = (base + g * GROUP) // GROUP
                        wide = table[rsl, lane].astype(jnp.float32) * sc[:, col : col + 1]
                        table[rsl, lane] = wide.astype(jnp.bfloat16)
            elif half == 0:
                for b in range(base, base + width, 256):
                    wgt_t[pl.ds(b, 256), :] = wgt[:, pl.ds(b, 256)].T

        def product(g, k):
            own, scr, tab, acc, base, width = chunks[k]
            for b in range(g * span, (g + 1) * span, 2 * tok):
                two = pl.ds(b, 2 * tok)
                part = dot_t(tab[:, pl.ds(base, width)], scr[two, pl.ds(base, width)])
                if firsts[k]:
                    acc[:, two] = part
                else:
                    acc[:, two] += part

        def local_stat(g):
            @pl.loop(0, n_y)
            def _(j):
                off = pl.multiple_of(j * tok, tok)
                sl = pl.ds(pl.multiple_of(g * span + j * tok, tok), tok)
                t_max = jnp.max(tlog[:, sl], axis=0, keepdims=True)
                s_max = jnp.max(slog[:, sl], axis=0, keepdims=True)
                te = jnp.exp(tlog[:, sl] - t_max)
                t_sum = jnp.sum(te, axis=0, keepdims=True)
                x_sum = jnp.sum(te * (tlog[:, sl] - slog[:, sl]), axis=0, keepdims=True)
                tlog[:, sl] = te
                se = jnp.exp(slog[:, sl] - s_max)
                s_sum = jnp.sum(se, axis=0, keepdims=True)
                slog[:, sl] = se
                stat[g, :, pl.ds(off, tok)] = jnp.concatenate(
                    [t_max, t_sum, x_sum, s_max, s_sum, jnp.zeros((3, tok), jnp.float32)],
                    axis=0,
                )

        def merge(parts):
            t_top = functools.reduce(jnp.maximum, [x[0:1] for x in parts])
            s_top = functools.reduce(jnp.maximum, [x[3:4] for x in parts])
            t_sum = x_sum = s_sum = 0.0
            for x in parts:
                t_w = jnp.exp(x[0:1] - t_top)
                t_sum += x[1:2] * t_w
                x_sum += x[2:3] * t_w
                s_sum += x[4:5] * jnp.exp(x[3:4] - s_top)
            return t_top, t_sum, x_sum, s_top, s_sum

        def a_copy(g, i):
            return rcopy(stat.at[g], in_a.at[g, i], a_r.at[g], peers_a[i])

        def b_copy(g, i):
            return rcopy(stat_b.at[g], in_b.at[g, i], b_r.at[g], peers_b[i])

        def send_a(g):
            local_stat(g)
            for i in reversed(range(len(peers_a))):
                launch(a_copy(g, i))

        def send_b(g):
            rcopy(in_a.at[g], in_a.at[g], a_r.at[g], X).wait_recv()
            stat_b[g] = jnp.concatenate(
                list(merge([stat[g]] + [in_a[g, i] for i in range(len(peers_a))]))
                + [jnp.zeros((3, span), jnp.float32)], axis=0
            )
            for i in range(len(peers_b)):
                launch(b_copy(g, i))

        def finish(g):
            rcopy(in_b.at[g], in_b.at[g], b_r.at[g], X).wait_recv()
            t_top, t_sum, x_sum, s_top, s_sum = merge(
                [stat_b[g]] + [in_b[g, i] for i in range(len(peers_b))]
            )
            t_lse = t_top + jnp.log(t_sum)
            s_lse = s_top + jnp.log(s_sum)
            fin[g] = jnp.concatenate(
                [
                    x_sum / t_sum - t_lse + s_lse,
                    jnp.exp(stat[g, 0:1] - t_lse),
                    jnp.exp(stat[g, 3:4] - s_lse),
                    jnp.zeros((5, span), jnp.float32),
                ],
                axis=0,
            )
            if g == c:
                kl_out[...] = fin[g, 0:1, pl.ds(pl.multiple_of(y * tok, tok), tok)]

            @pl.loop(0, n_y)
            def _(j):
                off = pl.multiple_of(j * tok, tok)
                sl = pl.ds(pl.multiple_of(g * span + j * tok, tok), tok)
                f = fin[g, :, pl.ds(off, tok)]
                grad[:, sl] = (
                    lsc[g * n_y + j][0:1] * (slog[:, sl] * f[2:3] - tlog[:, sl] * f[1:2])
                ).astype(jnp.bfloat16)

        def hidden(g, z):
            for pp in range(2):
                feat = wgt_t[pl.ds((2 * z + pp) * rv, rv), :]
                for yy in range(0, n_y, 2):
                    part = jnp.dot(
                        feat, grad[:, pl.ds(g * span + yy * tok, 2 * tok)],
                        preferred_element_type=jnp.float32,
                    )
                    for h in range(2):
                        one = part[:, h * tok : (h + 1) * tok]
                        if g == c:
                            mine[z, pp, yy + h] = one
                        else:
                            theirs[z, pp, yy + h] = one.astype(jnp.bfloat16)
            if g != c:
                launch(core_copy(z))

        def core_copy(z):
            return rcopy(theirs.at[z], core_in.at[z], cr.at[z], (v, mate))

        def y1_copy(z, o):
            to = 2 * lax.rem(y + o, n_y) + c
            return rcopy(y1s.at[z, o - 1], y1r.at[z, o - 1], r1r.at[z, o - 1], (v, to))

        def x1_copy(z):
            return rcopy(x1s.at[z], x1r.at[z], r2r.at[z, 0], (v_pair, d))

        def x2_copy(z):
            return rcopy(x2s.at[z - n_z1], x2r.at[z - n_z1], r1r.at[z, 0], (v_pair, d))

        def y2_copy(z, o):
            to = 2 * lax.rem(y + o, n_y) + c
            return rcopy(
                y2s.at[z - n_z1, o - 1], y2r.at[z - n_z1, o - 1], r2r.at[z, o - 1], (v, to),
            )

        def after_core(z):
            core_copy(z).wait_recv()
            if z < n_z1:
                for o in range(1, n_y):
                    to = lax.rem(y + o, n_y)
                    for pp in range(2):
                        y1s[z, o - 1, pp] = (
                            mine[z, pp, to] + core_in[z, pp, to].astype(jnp.float32)
                        ).astype(jnp.bfloat16)
                    launch(y1_copy(z, o))
            else:
                for yy in range(n_y):
                    x2s[z - n_z1, yy] = (
                        mine[z, 1 - p, yy] + core_in[z, 1 - p, yy].astype(jnp.float32)
                    ).astype(jnp.bfloat16)
                launch(x2_copy(z))

        def after_first(z):
            if z < n_z1:
                for o in range(1, n_y):
                    y1_copy(z, o).wait_recv()

                def total(which):
                    out = mine[z, which, y] + core_in[z, which, y].astype(jnp.float32)
                    for o in range(1, n_y):
                        out += y1r[z, o - 1, which].astype(jnp.float32)
                    return out

                x1s[z] = total(1 - p).astype(jnp.bfloat16)
                launch(x1_copy(z))
                zf[z] = total(p)
            else:
                x2_copy(z).wait_recv()

                def total(yy):
                    return (
                        mine[z, p, yy] + core_in[z, p, yy].astype(jnp.float32)
                        + x2r[z - n_z1, yy].astype(jnp.float32)
                    )

                for o in range(1, n_y):
                    y2s[z - n_z1, o - 1] = total(lax.rem(y + o, n_y)).astype(jnp.bfloat16)
                    launch(y2_copy(z, o))
                zf[z] = total(y)

        def z_copy(z):
            return rcopy(zs.at[z], zr.at[lax.rem(q + n_z - z, n_z) - 1], z_rs, (2 * z + p, d))

        def after_second(z):
            if z < n_z1:
                x1_copy(z).wait_recv()
                full = zf[z] + x1r[z].astype(jnp.float32)
            else:
                full = zf[z]
                for o in range(1, n_y):
                    y2_copy(z, o).wait_recv()
                    full += y2r[z - n_z1, o - 1].astype(jnp.float32)
            zf[z] = full
            zs[z] = full.astype(jnp.bfloat16)

            @pl.when(q != z)
            def _():
                z_copy(z).start()

        def weight_part(b):
            sl = pl.ds(b * 512, 512)
            gw_out[:, sl] = jnp.dot(
                grad[...], sh[:, sl], preferred_element_type=jnp.float32
            ).astype(jnp.bfloat16)

        def last():
            total = zf[q]
            rcopy(zr, zr, z_rs, X).wait_recv()
            for o in range(n_z - 1):
                total += zr[o].astype(jnp.float32)
            gh_out[...] = total.astype(jnp.bfloat16)

        def loss_wait():
            got = lsc.at[pl.ds(0, n_dp - 1)]
            rcopy(got, got, ls_r, X).wait_recv()

        def mate_copies():
            for i, (own, scr) in enumerate(((th_own, th), (sh_own, sh))):
                launch(rcopy(own, scr.at[pl.ds(block(c, y), tok)], pc_r.at[i], (v, mate)))

        def mate_arrived():
            for i, (own, scr) in enumerate(((th_own, th), (sh_own, sh))):
                rcopy(own, scr.at[pl.ds(block(1 - c, y), tok)], pc_r.at[i], (v, mate)).wait_recv()

        def named(name, fn, *args):
            with jax.named_scope(name + "_".join(str(x) for x in args if isinstance(x, int))):
                fn(*args)

        for dd in range(1, n_dp):
            launch(rcopy(loss_row, lsc.at[c * n_y + y], ls_r, (v, lax.rem(d + dd, n_dp))))
        far = [k for k in range(n_ch) if by_y[k]]

        def send_y(k):
            y_send(k, Y_A)
            if k == n_ch - 1:
                for kk in far:
                    y_send(kk, FAR)

        ops = {
            "p": lambda k: prepare(k, 0),
            "q": lambda k: prepare(k, 1),
            "s": send_y,
            "y": stage_y,
            "x": stage_xz,
            "f": stage_far,
            "d": lambda k: mate_wait(D_A, k),
            "m": lambda k: mate_wait(D_REST, k),
            "0": lambda k: product(0, k),
            "1": lambda k: product(1, k),
        }
        done = set()

        def play(steps, flush):
            todo = [(step[0], int(step[1:])) for step in steps]
            todo += [(name, k) for k in range(n_ch) for name in flush]
            for name, k in todo:
                if k < n_ch and (name, k) not in done:
                    done.add((name, k))
                    named(name, ops[name], k)

        if c == 0:
            play(("s0",), "")
            mate_copies()
            play(PLAY_A, "")
            for cp in own_loads:
                cp.wait()
            play(PLAY_B, "spqyxf0")
            named("send_a", send_a, 0)
            named("mate_arrived", mate_arrived)
            play(PLAY_C, "")
            named("send_b", send_b, 0)
            play(PLAY_I, "dm1")
            named("send_a", send_a, 1)
            loss_wait()
            named("finish", finish, 0)
            for i, z in enumerate(order):
                named("hidden", hidden, 0, z)
                if i >= 1:
                    named("after_core", after_core, order[i - 1])
            named("after_core", after_core, order[-1])
            named("send_b", send_b, 1)
            named("finish", finish, 1)
            for z in order:
                named("hidden", hidden, 1, z)
            for z in order:
                named("after_first", after_first, z)
            for b in range(n_gw):
                named("weight", weight_part, b)
            for z in order:
                named("after_second", after_second, z)
            named("last", last)
        else:
            mate_copies()
            play(PLAY_D, "pq")
            for cp in own_loads:
                cp.wait()
            play(PLAY_E, "ds")
            named("mate_arrived", mate_arrived)
            play(PLAY_F, "m0")
            named("send_a", send_a, 0)
            play(PLAY_G, "")
            named("send_b", send_b, 0)
            play(PLAY_H, "yxf1")
            named("send_a", send_a, 1)
            loss_wait()
            named("finish", finish, 0)
            for z in order:
                named("hidden", hidden, 0, z)
            named("send_b", send_b, 1)
            named("finish", finish, 1)
            for i, z in enumerate(order):
                named("hidden", hidden, 1, z)
                if i >= 1:
                    named("after_core", after_core, order[i - 1])
            named("after_core", after_core, order[-1])
            for b in range(n_gw):
                named("weight", weight_part, b)
            for z in order:
                named("after_first", after_first, z)
            for z in order:
                named("after_second", after_second, z)
            named("last", last)

        for cp in sends:
            cp.wait_send()
        for o in range(1, n_z):
            z_copy(lax.rem(q + o, n_z)).wait_send()

    for which in range(2):
        pl.when(core == which)(functools.partial(run, which))


def hand_over(kl, gh, gw):
    parts = 4
    step = gw.shape[0] // parts

    def move(kl_in, gh_in, gw_in, kl_to, gh_to, gw_to, sem):
        plan = [(gh_in, gh_to), (kl_in, kl_to)]
        for i in range(parts):
            sl = pl.ds(i * step, step)
            plan.append((gw_in.at[sl], gw_to.at[sl]))
        writes = [pltpu.make_async_copy(a, b, sem.at[i]) for i, (a, b) in enumerate(plan)]
        for cp in writes:
            cp.start()
        for cp in writes:
            cp.wait()

    spec = pl.BlockSpec(memory_space=pl.ANY)
    arrays = (kl, gh, gw)
    return pl.pallas_call(
        move,
        out_shape=tuple(jax.ShapeDtypeStruct(a.shape, a.dtype) for a in arrays),
        in_specs=[pl.BlockSpec(memory_space=pltpu.VMEM)] * 3,
        out_specs=(spec,) * 3,
        scratch_shapes=[pltpu.SemaphoreType.DMA((parts + 2,))],
        compiler_params=pltpu.CompilerParams(vmem_limit_bytes=4 * 1024 * 1024),
        name="hand_over",
    )(*arrays)


def solution(mesh):
    n_vocab, n_dp = mesh.shape["vocab"], mesh.shape["dp"]

    def local(th_own, sh_own, codes, scales, weight, loss_scale):
        tok, dt = th_own.shape
        ds_ = sh_own.shape[1]
        rows = codes.shape[0]
        n_tok = tok * n_dp
        n_y, n_z = n_dp // 2, n_vocab // 2
        n_off, n_z1 = n_y - 1, n_z // 2
        n_z2 = n_z - n_z1
        rv = ds_ // n_vocab
        n_ch = len(chunk_widths(dt, True)) + len(chunk_widths(ds_, False))
        span = n_y * tok
        n_a, n_b = 2 * n_dp - 1, n_z - 1
        bf, f32 = jnp.bfloat16, jnp.float32
        V, D = pltpu.VMEM, pltpu.SemaphoreType.DMA
        any_spec = pl.BlockSpec(memory_space=pl.ANY)
        vm_spec = pl.BlockSpec(memory_space=pltpu.VMEM)
        kl, gh, gw = pl.pallas_call(
            functools.partial(kernel, n_vocab, n_dp),
            out_shape=(
                pltpu.VMEM((1, tok), f32),
                pltpu.VMEM((rv, tok), bf),
                pltpu.VMEM((rows, ds_), bf),
            ),
            in_specs=[any_spec, any_spec, any_spec, vm_spec, any_spec, vm_spec],
            out_specs=(vm_spec, vm_spec, vm_spec),
            scratch_shapes=[
                V((n_tok, dt), bf), V((n_tok, ds_), bf), V((rows, dt), bf), V((rows, ds_), bf),
                V((ds_, rows), bf), V((rows, n_tok), f32), V((rows, n_tok), f32),
                V((n_dp, 8, tok), f32), V((2, 8, span), f32), V((2, 8, span), f32),
                V((2, 8, span), f32), V((2, n_a, 8, span), f32), V((2, n_b, 8, span), f32),
                V((rows, n_tok), bf),
                V((n_z, 2, n_y, rv, tok), f32), V((n_z, 2, n_y, rv, tok), bf),
                V((n_z, 2, n_y, rv, tok), bf),
                V((n_z1, n_off, 2, rv, tok), bf), V((n_z1, n_off, 2, rv, tok), bf),
                V((n_z1, rv, tok), bf), V((n_z1, rv, tok), bf),
                V((n_z2, n_y, rv, tok), bf), V((n_z2, n_y, rv, tok), bf),
                V((n_z2, n_off, rv, tok), bf), V((n_z2, n_off, rv, tok), bf),
                V((n_z, rv, tok), bf), V((n_z - 1, rv, tok), bf), V((n_z, rv, tok), f32),
                V((rows, -(-scales.shape[1] // 8) * 8), f32), V((8, tok), f32),
                D((n_ch + 2,)), D((2,)), D((6, n_off, n_ch)), D, D, D((2,)), D((2,)),
                D((n_z,)), D((n_z, n_off)), D((n_z, n_off)), D,
            ],
            compiler_params=pltpu.CompilerParams(
                collective_id=0, has_side_effects=True, vmem_limit_bytes=56 * 1024 * 1024
            ),
            name="distill",
        )(th_own, sh_own, codes, scales.T, weight, loss_scale)
        kl, gh, gw = hand_over(kl, gh, gw)
        return kl.reshape(tok), gh.T, gw

    in_specs = (
        P("dp", None),
        P("dp", None),
        P(("vocab", "dp"), None),
        P(("vocab", "dp"), None),
        P(("vocab", "dp"), None),
        P("dp"),
    )
    out_specs = (P("dp"), P("dp", "vocab"), P(("vocab", "dp"), None))
    return jax.shard_map(local, mesh=mesh, in_specs=in_specs, out_specs=out_specs, check_vma=False)
```

```python
import functools

import jax
import jax.numpy as jnp
from jax import lax
from jax.experimental import pallas as pl
from jax.experimental.pallas import tpu as pltpu
from jax.sharding import PartitionSpec as P

GROUP = 128
LANE = 128
MESH = pl.DeviceIdType.MESH

PLAY_A = (
    "s1", "s2", "s3", "s4", "s5", "p0", "q0", "p1", "q1", "p2",
)
PLAY_B = (
    "y0", "q2", "y1", "p3", "y2", "q3", "y3", "x0", "y4", "x1", "y5", "p4", "p5", "x2", "f0",
    "00", "x3", "f3", "03", "f1", "01", "x4", "f4", "04", "x5", "f5", "05", "f2", "02",
)
PLAY_C = (
    "d0", "m0", "10", "d1", "m1", "11", "d2", "m2", "12",
)
PLAY_I = (
    "d3", "m3", "13", "d4", "m4", "14", "d5", "m5", "15",
)
PLAY_D = (
    "p0", "q0", "p1", "q1", "p2", "q2", "p3", "q3", "d0", "s0", "d1", "s1", "p4", "d2", "s2",
    "p5",
)
PLAY_E = (
    "d3", "s3", "s4", "s5", "y0", "d4", "y1", "d5",
)
PLAY_F = (
    "x0", "y2", "m0", "00", "m3", "03", "m1", "01", "y3", "x1", "y4", "m4", "04", "x2", "f0",
    "y5", "m5", "05", "m2", "02",
)
PLAY_G = (
    "x3", "10", "f1", "x4", "11", "f2", "12", "x5", "f3",
)
PLAY_H = (
    "f4", "13", "f5", "14", "15",
)


def dot_t(left_rows, right_rows):
    return lax.dot_general(
        left_rows, right_rows, (((1,), (1,)), ((), ())), preferred_element_type=jnp.float32
    )


def chunk_widths(cols, lead):
    units = cols // 256
    head = [3] if lead and units > 3 else []
    rest = units - sum(head)
    per = max(k for k in (1, 2, 3, 5, 6, 7) if rest % k == 0)
    return [256 * n for n in head + [per] * (rest // per)]


def kernel(
    n_vocab, n_dp,
    th_own, sh_own, codes, scales, weight, loss_in,
    kl_out, gh_out, gw_out,
    th, sh, table, wgt, wgt_t, tlog, slog, lsc, stat, stat_b, fin, in_a, in_b,
    grad, mine, theirs, core_in,
    y1s, y1r, x1s, x1r, x2s, x2r, y2s, y2r, zs, zr, zf,
    sc_rows, loss_row, ld_sem, pc_r, hop_r, sent, ls_r, a_r, b_r, cr, r1r, r2r, z_rs,
):
    v, d = lax.axis_index("vocab"), lax.axis_index("dp")
    core, y = lax.rem(d, 2), lax.div(d, 2)
    p, q = lax.rem(v, 2), lax.div(v, 2)
    n_y, n_z = n_dp // 2, n_vocab // 2
    v_pair = 2 * q + 1 - p
    r = lax.rem(q, 2)
    v_quad = 2 * (q + 1 - 2 * r) + p
    tok = th_own.shape[0]
    rv = zr.shape[1]
    n_z1 = n_z // 2
    span = n_y * tok
    quarter = tok // 4

    def rcopy(src, dst, recv, dev):
        return pltpu.make_async_remote_copy(
            src_ref=src, dst_ref=dst, send_sem=sent, recv_sem=recv,
            device_id=dev, device_id_type=MESH,
        )

    peers_a = []
    for dv in range(2):
        for dd in range(n_dp):
            if dv or dd:
                peers_a.append((v if dv == 0 else v_pair, lax.rem(d + dd, n_dp)))
    peers_b = [(2 * lax.rem(q + o, n_z) + p, d) for o in range(1, n_z)]
    barrier = pltpu.get_barrier_semaphore()
    for peer in peers_a + peers_b:
        pl.semaphore_signal(barrier, inc=1, device_id=peer, device_id_type=MESH)

    chunks = []
    for own, scr, tab, acc in ((th_own, th, table, tlog), (sh_own, sh, wgt, slog)):
        base = 0
        for width in chunk_widths(own.shape[1], tab is table):
            chunks.append((own, scr, tab, acc, base, width))
            base += width
    n_ch = len(chunks)
    firsts = [k == 0 or chunks[k][3] is not chunks[k - 1][3] for k in range(n_ch)]
    by_y = [False] * n_ch
    room = sum(ch[5] for ch in chunks) * 55 // 100
    for k in reversed(range(n_ch)):
        room -= chunks[k][5]
        if room < 0:
            break
        by_y[k] = True

    def block(g, yy):
        return pl.multiple_of((g * n_y + yy) * tok, tok)

    my_rows = pl.ds(pl.multiple_of((core * n_y + y) * tok, tok), tok)
    loads = []
    for k, (own, scr, tab, acc, base, width) in enumerate(chunks):
        src = codes if tab is table else weight
        cp = pltpu.make_async_copy(
            src.at[:, pl.ds(base, width)], tab.at[:, pl.ds(base, width)], ld_sem.at[k]
        )
        cp.start()
        loads.append(cp)
    own_loads = [
        pltpu.make_async_copy(th_own, th.at[my_rows], ld_sem.at[n_ch]),
        pltpu.make_async_copy(sh_own, sh.at[my_rows], ld_sem.at[n_ch + 1]),
    ]
    for cp in own_loads:
        cp.start()
    groups = scales.shape[0]
    pad = jnp.zeros((sc_rows.shape[1] - groups, LANE), jnp.float32)
    for b in range(0, scales.shape[1], LANE):
        sc_rows[pl.ds(b, LANE), :] = jnp.concatenate(
            [scales[:, pl.ds(b, LANE)], pad], axis=0
        ).T
    loss_row[...] = jnp.broadcast_to(
        loss_in[...].astype(jnp.float32).reshape(1, tok), loss_row.shape
    )
    lsc[core * n_y + y] = loss_row[...]
    with jax.named_scope("barrier"):
        pl.semaphore_wait(barrier, len(peers_a) + len(peers_b))

    A, B, C, E = 2 * r + p, 2 * r + 1 - p, 2 * (1 - r) + p, 2 * (1 - r) + 1 - p
    Y_A, X_A, Z_A, FAR, D_A, D_REST = range(6)
    order = []
    for i in range(n_z1):
        order += [i, n_z1 + i]
    order += [i for i in range(n_z) if i not in order]
    n_gw = sh.shape[1] // 512

    def run(c):
        mate = 2 * y + 1 - c
        X, Z = (v_pair, d), (v_quad, d)
        sends = []

        def launch(cp):
            cp.start()
            sends.append(cp)

        def region(g, k, yy, piece, half=None):
            scr, base, width = chunks[k][1], chunks[k][4], chunks[k][5]
            first, size = block(g, yy) + piece * quarter, quarter
            if half is not None:
                size = quarter // 2
                first += half * size
            return scr.at[pl.ds(pl.multiple_of(first, size), size), pl.ds(base, width)]

        def came(o):
            return lax.rem(y + n_y - o, n_y)

        def y_send(k, kind):
            own, base, width = chunks[k][0], chunks[k][4], chunks[k][5]
            piece = A if kind == Y_A else E
            src = own.at[
                pl.ds(pl.multiple_of(piece * quarter, quarter), quarter), pl.ds(base, width)
            ]
            for o in range(1, n_y):
                to = 2 * lax.rem(y + o, n_y) + c
                launch(rcopy(src, region(c, k, y, piece), hop_r.at[kind, o - 1, k], (v, to)))

        def hop(kind, k, o, piece, dev, half=None):
            ref = region(c, k, came(o), piece, half)
            return rcopy(ref, ref, hop_r.at[kind, o - 1, k], dev)

        def to_mate(kind, k, o, piece):
            launch(hop(kind, k, o, piece, (v, mate)))

        def stage_y(k):
            for o in range(1, n_y):
                hop(Y_A, k, o, A, X).wait_recv()
                launch(hop(X_A, k, o, A, X))
                launch(hop(Z_A, k, o, A, Z))
                to_mate(D_A, k, o, A)

        def stage_xz(k):
            for o in range(1, n_y):
                hop(X_A, k, o, B, X).wait_recv()
                if not by_y[k]:
                    launch(hop(FAR, k, o, B, Z, 1))
                to_mate(D_REST, k, o, B)
                hop(Z_A, k, o, C, Z).wait_recv()
                if not by_y[k]:
                    launch(hop(FAR, k, o, C, X, 0))
                to_mate(D_REST, k, o, C)

        def stage_far(k):
            for o in range(1, n_y):
                hop(FAR, k, o, E, X).wait_recv()
                to_mate(D_REST, k, o, E)

        def mate_wait(kind, k):
            scr, base, width = chunks[k][1], chunks[k][4], chunks[k][5]
            size = quarter if kind == D_A else 3 * quarter
            for o in range(1, n_y):
                ref = scr.at[pl.ds(block(1 - c, came(o)), size), pl.ds(base, width)]
                rcopy(ref, ref, hop_r.at[kind, o - 1, k], X).wait_recv()

        def prepare(k, half):
            own, scr, tab, acc, base, width = chunks[k]
            if half == 0:
                loads[k].wait()
            steps = table.shape[0] // 128
            if tab is table:
                @pl.loop(half * steps, (half + 1) * steps)
                def _(i):
                    rsl = pl.ds(pl.multiple_of(i * 64, 64), 64)
                    sc = sc_rows[rsl, :]
                    for g in range(width // GROUP):
                        lane = pl.ds(base + g * GROUP, GROUP)
                        col = (base + g * GROUP) // GROUP
                        wide = table[rsl, lane].astype(jnp.float32) * sc[:, col : col + 1]
                        table[rsl, lane] = wide.astype(jnp.bfloat16)
            elif half == 0:
                for b in range(base, base + width, 256):
                    wgt_t[pl.ds(b, 256), :] = wgt[:, pl.ds(b, 256)].T

        def product(g, k):
            own, scr, tab, acc, base, width = chunks[k]
            for b in range(g * span, (g + 1) * span, 2 * tok):
                two = pl.ds(b, 2 * tok)
                half = tab.shape[0] // 2
                for h in range(2):
                    top = pl.ds(h * half, half)
                    part = dot_t(tab[top, pl.ds(base, width)], scr[two, pl.ds(base, width)])
                    if firsts[k]:
                        acc[top, two] = part
                    else:
                        acc[top, two] += part

        def local_stat(g):
            @pl.loop(0, n_y)
            def _(j):
                off = pl.multiple_of(j * tok, tok)
                sl = pl.ds(pl.multiple_of(g * span + j * tok, tok), tok)
                t_max = jnp.max(tlog[:, sl], axis=0, keepdims=True)
                s_max = jnp.max(slog[:, sl], axis=0, keepdims=True)
                te = jnp.exp(tlog[:, sl] - t_max)
                t_sum = jnp.sum(te, axis=0, keepdims=True)
                x_sum = jnp.sum(te * (tlog[:, sl] - slog[:, sl]), axis=0, keepdims=True)
                tlog[:, sl] = te
                se = jnp.exp(slog[:, sl] - s_max)
                s_sum = jnp.sum(se, axis=0, keepdims=True)
                slog[:, sl] = se
                stat[g, :, pl.ds(off, tok)] = jnp.concatenate(
                    [t_max, t_sum, x_sum, s_max, s_sum, jnp.zeros((3, tok), jnp.float32)],
                    axis=0,
                )

        def merge(parts):
            t_top = functools.reduce(jnp.maximum, [x[0:1] for x in parts])
            s_top = functools.reduce(jnp.maximum, [x[3:4] for x in parts])
            t_sum = x_sum = s_sum = 0.0
            for x in parts:
                t_w = jnp.exp(x[0:1] - t_top)
                t_sum += x[1:2] * t_w
                x_sum += x[2:3] * t_w
                s_sum += x[4:5] * jnp.exp(x[3:4] - s_top)
            return t_top, t_sum, x_sum, s_top, s_sum

        def a_copy(g, i):
            return rcopy(stat.at[g], in_a.at[g, i], a_r.at[g], peers_a[i])

        def b_copy(g, i):
            return rcopy(stat_b.at[g], in_b.at[g, i], b_r.at[g], peers_b[i])

        def send_a(g):
            local_stat(g)
            for i in reversed(range(len(peers_a))):
                launch(a_copy(g, i))

        def send_b(g):
            rcopy(in_a.at[g], in_a.at[g], a_r.at[g], X).wait_recv()
            stat_b[g] = jnp.concatenate(
                list(merge([stat[g]] + [in_a[g, i] for i in range(len(peers_a))]))
                + [jnp.zeros((3, span), jnp.float32)], axis=0
            )
            for i in range(len(peers_b)):
                launch(b_copy(g, i))

        def finish(g):
            rcopy(in_b.at[g], in_b.at[g], b_r.at[g], X).wait_recv()
            t_top, t_sum, x_sum, s_top, s_sum = merge(
                [stat_b[g]] + [in_b[g, i] for i in range(len(peers_b))]
            )
            t_lse = t_top + jnp.log(t_sum)
            s_lse = s_top + jnp.log(s_sum)
            fin[g] = jnp.concatenate(
                [
                    x_sum / t_sum - t_lse + s_lse,
                    jnp.exp(stat[g, 0:1] - t_lse),
                    jnp.exp(stat[g, 3:4] - s_lse),
                    jnp.zeros((5, span), jnp.float32),
                ],
                axis=0,
            )
            if g == c:
                kl_out[...] = fin[g, 0:1, pl.ds(pl.multiple_of(y * tok, tok), tok)]

            @pl.loop(0, n_y)
            def _(j):
                off = pl.multiple_of(j * tok, tok)
                sl = pl.ds(pl.multiple_of(g * span + j * tok, tok), tok)
                f = fin[g, :, pl.ds(off, tok)]
                grad[:, sl] = (
                    lsc[g * n_y + j][0:1] * (slog[:, sl] * f[2:3] - tlog[:, sl] * f[1:2])
                ).astype(jnp.bfloat16)

        def hidden(g, z):
            for pp in range(2):
                feat = wgt_t[pl.ds((2 * z + pp) * rv, rv), :]
                for yy in range(0, n_y, 2):
                    part = jnp.dot(
                        feat, grad[:, pl.ds(g * span + yy * tok, 2 * tok)],
                        preferred_element_type=jnp.float32,
                    )
                    for h in range(2):
                        one = part[:, h * tok : (h + 1) * tok]
                        if g == c:
                            mine[z, pp, yy + h] = one
                        else:
                            theirs[z, pp, yy + h] = one.astype(jnp.bfloat16)
            if g != c:
                launch(core_copy(z))

        def core_copy(z):
            return rcopy(theirs.at[z], core_in.at[z], cr.at[z], (v, mate))

        def y1_copy(z, o):
            to = 2 * lax.rem(y + o, n_y) + c
            return rcopy(y1s.at[z, o - 1], y1r.at[z, o - 1], r1r.at[z, o - 1], (v, to))

        def x1_copy(z):
            return rcopy(x1s.at[z], x1r.at[z], r2r.at[z, 0], (v_pair, d))

        def x2_copy(z):
            return rcopy(x2s.at[z - n_z1], x2r.at[z - n_z1], r1r.at[z, 0], (v_pair, d))

        def y2_copy(z, o):
            to = 2 * lax.rem(y + o, n_y) + c
            return rcopy(
                y2s.at[z - n_z1, o - 1], y2r.at[z - n_z1, o - 1], r2r.at[z, o - 1], (v, to),
            )

        def after_core(z):
            core_copy(z).wait_recv()
            if z < n_z1:
                for o in range(1, n_y):
                    to = lax.rem(y + o, n_y)
                    for pp in range(2):
                        y1s[z, o - 1, pp] = (
                            mine[z, pp, to] + core_in[z, pp, to].astype(jnp.float32)
                        ).astype(jnp.bfloat16)
                    launch(y1_copy(z, o))
            else:
                for yy in range(n_y):
                    x2s[z - n_z1, yy] = (
                        mine[z, 1 - p, yy] + core_in[z, 1 - p, yy].astype(jnp.float32)
                    ).astype(jnp.bfloat16)
                launch(x2_copy(z))

        def after_first(z):
            if z < n_z1:
                for o in range(1, n_y):
                    y1_copy(z, o).wait_recv()

                def total(which):
                    out = mine[z, which, y] + core_in[z, which, y].astype(jnp.float32)
                    for o in range(1, n_y):
                        out += y1r[z, o - 1, which].astype(jnp.float32)
                    return out

                x1s[z] = total(1 - p).astype(jnp.bfloat16)
                launch(x1_copy(z))
                zf[z] = total(p)
            else:
                x2_copy(z).wait_recv()

                def total(yy):
                    return (
                        mine[z, p, yy] + core_in[z, p, yy].astype(jnp.float32)
                        + x2r[z - n_z1, yy].astype(jnp.float32)
                    )

                for o in range(1, n_y):
                    y2s[z - n_z1, o - 1] = total(lax.rem(y + o, n_y)).astype(jnp.bfloat16)
                    launch(y2_copy(z, o))
                zf[z] = total(y)

        def z_copy(z):
            return rcopy(zs.at[z], zr.at[lax.rem(q + n_z - z, n_z) - 1], z_rs, (2 * z + p, d))

        def after_second(z):
            if z < n_z1:
                x1_copy(z).wait_recv()
                full = zf[z] + x1r[z].astype(jnp.float32)
            else:
                full = zf[z]
                for o in range(1, n_y):
                    y2_copy(z, o).wait_recv()
                    full += y2r[z - n_z1, o - 1].astype(jnp.float32)
            zf[z] = full
            zs[z] = full.astype(jnp.bfloat16)

            @pl.when(q != z)
            def _():
                z_copy(z).start()

        def weight_part(b):
            sl = pl.ds(b * 512, 512)
            gw_out[:, sl] = jnp.dot(
                grad[...], sh[:, sl], preferred_element_type=jnp.float32
            ).astype(jnp.bfloat16)

        def last():
            total = zf[q]
            rcopy(zr, zr, z_rs, X).wait_recv()
            for o in range(n_z - 1):
                total += zr[o].astype(jnp.float32)
            gh_out[...] = total.astype(jnp.bfloat16)

        def loss_wait():
            got = lsc.at[pl.ds(0, n_dp - 1)]
            rcopy(got, got, ls_r, X).wait_recv()

        def mate_copies():
            for i, (own, scr) in enumerate(((th_own, th), (sh_own, sh))):
                launch(rcopy(own, scr.at[pl.ds(block(c, y), tok)], pc_r.at[i], (v, mate)))

        def mate_arrived():
            for i, (own, scr) in enumerate(((th_own, th), (sh_own, sh))):
                rcopy(own, scr.at[pl.ds(block(1 - c, y), tok)], pc_r.at[i], (v, mate)).wait_recv()

        def named(name, fn, *args):
            with jax.named_scope(name + "_".join(str(x) for x in args if isinstance(x, int))):
                fn(*args)

        for dd in range(1, n_dp):
            launch(rcopy(loss_row, lsc.at[c * n_y + y], ls_r, (v, lax.rem(d + dd, n_dp))))
        far = [k for k in range(n_ch) if by_y[k]]

        def send_y(k):
            y_send(k, Y_A)
            if k == n_ch - 1:
                for kk in far:
                    y_send(kk, FAR)

        ops = {
            "p": lambda k: prepare(k, 0),
            "q": lambda k: prepare(k, 1),
            "s": send_y,
            "y": stage_y,
            "x": stage_xz,
            "f": stage_far,
            "d": lambda k: mate_wait(D_A, k),
            "m": lambda k: mate_wait(D_REST, k),
            "0": lambda k: product(0, k),
            "1": lambda k: product(1, k),
        }
        done = set()

        def play(steps, flush):
            todo = [(step[0], int(step[1:])) for step in steps]
            todo += [(name, k) for k in range(n_ch) for name in flush]
            for name, k in todo:
                if k < n_ch and (name, k) not in done:
                    done.add((name, k))
                    named(name, ops[name], k)

        if c == 0:
            play(("s0",), "")
            mate_copies()
            play(PLAY_A, "")
            for cp in own_loads:
                cp.wait()
            play(PLAY_B, "spqyxf0")
            named("send_a", send_a, 0)
            named("mate_arrived", mate_arrived)
            play(PLAY_C, "")
            named("send_b", send_b, 0)
            play(PLAY_I, "dm1")
            named("send_a", send_a, 1)
            loss_wait()
            named("finish", finish, 0)
            for i, z in enumerate(order):
                named("hidden", hidden, 0, z)
                if i >= 1:
                    named("after_core", after_core, order[i - 1])
            named("after_core", after_core, order[-1])
            named("send_b", send_b, 1)
            for z in order[:2]:
                named("after_first", after_first, z)
            named("finish", finish, 1)
            for z in order:
                named("hidden", hidden, 1, z)
            for z in order[2:]:
                named("after_first", after_first, z)
            for b in range(n_gw):
                named("weight", weight_part, b)
            for z in order:
                named("after_second", after_second, z)
            named("last", last)
        else:
            mate_copies()
            play(PLAY_D, "pq")
            for cp in own_loads:
                cp.wait()
            play(PLAY_E, "ds")
            named("mate_arrived", mate_arrived)
            play(PLAY_F, "m0")
            named("send_a", send_a, 0)
            play(PLAY_G, "")
            named("send_b", send_b, 0)
            play(PLAY_H, "yxf1")
            named("send_a", send_a, 1)
            loss_wait()
            named("finish", finish, 0)
            for z in order:
                named("hidden", hidden, 0, z)
            named("send_b", send_b, 1)
            named("finish", finish, 1)
            for i, z in enumerate(order):
                named("hidden", hidden, 1, z)
                if i >= 1:
                    named("after_core", after_core, order[i - 1])
            named("after_core", after_core, order[-1])
            for b in range(n_gw):
                named("weight", weight_part, b)
            for z in order:
                named("after_first", after_first, z)
            for z in order:
                named("after_second", after_second, z)
            named("last", last)

        for cp in sends:
            cp.wait_send()
        for o in range(1, n_z):
            z_copy(lax.rem(q + o, n_z)).wait_send()

    for which in range(2):
        pl.when(core == which)(functools.partial(run, which))


def hand_over(kl, gh, gw):
    parts = 4
    step = gw.shape[0] // parts

    def move(kl_in, gh_in, gw_in, kl_to, gh_to, gw_to, sem):
        plan = [(gh_in, gh_to), (kl_in, kl_to)]
        for i in range(parts):
            sl = pl.ds(i * step, step)
            plan.append((gw_in.at[sl], gw_to.at[sl]))
        writes = [pltpu.make_async_copy(a, b, sem.at[i]) for i, (a, b) in enumerate(plan)]
        for cp in writes:
            cp.start()
        for cp in writes:
            cp.wait()

    spec = pl.BlockSpec(memory_space=pl.ANY)
    arrays = (kl, gh, gw)
    return pl.pallas_call(
        move,
        out_shape=tuple(jax.ShapeDtypeStruct(a.shape, a.dtype) for a in arrays),
        in_specs=[pl.BlockSpec(memory_space=pltpu.VMEM)] * 3,
        out_specs=(spec,) * 3,
        scratch_shapes=[pltpu.SemaphoreType.DMA((parts + 2,))],
        compiler_params=pltpu.CompilerParams(vmem_limit_bytes=4 * 1024 * 1024),
        name="hand_over",
    )(*arrays)


def solution(mesh):
    n_vocab, n_dp = mesh.shape["vocab"], mesh.shape["dp"]

    def local(th_own, sh_own, codes, scales, weight, loss_scale):
        tok, dt = th_own.shape
        ds_ = sh_own.shape[1]
        rows = codes.shape[0]
        n_tok = tok * n_dp
        n_y, n_z = n_dp // 2, n_vocab // 2
        n_off, n_z1 = n_y - 1, n_z // 2
        n_z2 = n_z - n_z1
        rv = ds_ // n_vocab
        n_ch = len(chunk_widths(dt, True)) + len(chunk_widths(ds_, False))
        span = n_y * tok
        n_a, n_b = 2 * n_dp - 1, n_z - 1
        bf, f32 = jnp.bfloat16, jnp.float32
        V, D = pltpu.VMEM, pltpu.SemaphoreType.DMA
        any_spec = pl.BlockSpec(memory_space=pl.ANY)
        vm_spec = pl.BlockSpec(memory_space=pltpu.VMEM)
        kl, gh, gw = pl.pallas_call(
            functools.partial(kernel, n_vocab, n_dp),
            out_shape=(
                pltpu.VMEM((1, tok), f32),
                pltpu.VMEM((rv, tok), bf),
                pltpu.VMEM((rows, ds_), bf),
            ),
            in_specs=[any_spec, any_spec, any_spec, vm_spec, any_spec, vm_spec],
            out_specs=(vm_spec, vm_spec, vm_spec),
            scratch_shapes=[
                V((n_tok, dt), bf), V((n_tok, ds_), bf), V((rows, dt), bf), V((rows, ds_), bf),
                V((ds_, rows), bf), V((rows, n_tok), f32), V((rows, n_tok), f32),
                V((n_dp, 8, tok), f32), V((2, 8, span), f32), V((2, 8, span), f32),
                V((2, 8, span), f32), V((2, n_a, 8, span), f32), V((2, n_b, 8, span), f32),
                V((rows, n_tok), bf),
                V((n_z, 2, n_y, rv, tok), f32), V((n_z, 2, n_y, rv, tok), bf),
                V((n_z, 2, n_y, rv, tok), bf),
                V((n_z1, n_off, 2, rv, tok), bf), V((n_z1, n_off, 2, rv, tok), bf),
                V((n_z1, rv, tok), bf), V((n_z1, rv, tok), bf),
                V((n_z2, n_y, rv, tok), bf), V((n_z2, n_y, rv, tok), bf),
                V((n_z2, n_off, rv, tok), bf), V((n_z2, n_off, rv, tok), bf),
                V((n_z, rv, tok), bf), V((n_z - 1, rv, tok), bf), V((n_z, rv, tok), f32),
                V((rows, -(-scales.shape[1] // 8) * 8), f32), V((8, tok), f32),
                D((n_ch + 2,)), D((2,)), D((6, n_off, n_ch)), D, D, D((2,)), D((2,)),
                D((n_z,)), D((n_z, n_off)), D((n_z, n_off)), D,
            ],
            compiler_params=pltpu.CompilerParams(
                collective_id=0, has_side_effects=True, vmem_limit_bytes=56 * 1024 * 1024
            ),
            name="distill",
        )(th_own, sh_own, codes, scales.T, weight, loss_scale)
        kl, gh, gw = hand_over(kl, gh, gw)
        return kl.reshape(tok), gh.T, gw

    in_specs = (
        P("dp", None),
        P("dp", None),
        P(("vocab", "dp"), None),
        P(("vocab", "dp"), None),
        P(("vocab", "dp"), None),
        P("dp"),
    )
    out_specs = (P("dp"), P("dp", "vocab"), P(("vocab", "dp"), None))
    return jax.shard_map(local, mesh=mesh, in_specs=in_specs, out_specs=out_specs, check_vma=False)
```

```python
import functools

import jax
import jax.numpy as jnp
from jax import lax
from jax.experimental import pallas as pl
from jax.experimental.pallas import tpu as pltpu
from jax.sharding import PartitionSpec as P

GROUP = 128
LANE = 128
MESH = pl.DeviceIdType.MESH

PLAY_A = (
    "s1", "s2", "s3", "s4", "s5", "p0", "q0", "p1", "q1", "p2",
)
PLAY_B = (
    "y0", "q2", "y1", "p3", "y2", "q3", "y3", "x0", "y4", "x1", "y5", "p4", "p5", "x2", "f0",
    "00", "x3", "f3", "03", "f1", "01", "x4", "f4", "04", "x5", "f5", "05", "f2", "02",
)
PLAY_C = (
    "d0", "m0", "10", "d1", "m1", "11", "d2", "m2", "12",
)
PLAY_I = (
    "d3", "m3", "13", "d4", "m4", "14", "d5", "m5", "15",
)
PLAY_D = (
    "p0", "q0", "p1", "q1", "p2", "q2", "p3", "q3", "d0", "s0", "d1", "s1", "p4", "d2", "s2",
    "p5",
)
PLAY_E = (
    "d3", "s3", "s4", "s5", "y0", "d4", "y1", "d5",
)
PLAY_F = (
    "x0", "y2", "m0", "00", "m3", "03", "m1", "01", "y3", "x1", "y4", "m4", "04", "x2", "f0",
    "y5", "m5", "05", "m2", "02",
)
PLAY_G = (
    "x3", "10", "f1", "x4", "11", "f2", "12", "x5", "f3",
)
PLAY_H = (
    "f4", "13", "f5", "14", "15",
)


def dot_t(left_rows, right_rows):
    return lax.dot_general(
        left_rows, right_rows, (((1,), (1,)), ((), ())), preferred_element_type=jnp.float32
    )


def chunk_widths(cols, lead):
    units = cols // 256
    head = [3] if lead and units > 3 else []
    rest = units - sum(head)
    per = max(k for k in (1, 2, 3, 5, 6, 7) if rest % k == 0)
    return [256 * n for n in head + [per] * (rest // per)]


def kernel(
    n_vocab, n_dp,
    th_own, sh_own, codes, scales, weight, loss_in,
    kl_out, gh_out, gw_out,
    th, sh, table, wgt, wgt_t, tlog, slog, lsc, stat, stat_b, fin, in_a, in_b,
    grad, grad_m, wgt_m, tl_m, sl_m, mine,
    y1s, y1r, x1s, x1r, x2s, x2r, y2s, y2r, zs, zr, zf,
    sc_rows, loss_row, ld_sem, pc_r, hop_r, sent, ls_r, a_r, b_r, w_r, e_r, r1r, r2r, z_rs,
):
    v, d = lax.axis_index("vocab"), lax.axis_index("dp")
    core, y = lax.rem(d, 2), lax.div(d, 2)
    p, q = lax.rem(v, 2), lax.div(v, 2)
    n_y, n_z = n_dp // 2, n_vocab // 2
    v_pair = 2 * q + 1 - p
    r = lax.rem(q, 2)
    v_quad = 2 * (q + 1 - 2 * r) + p
    tok = th_own.shape[0]
    rv = zr.shape[1]
    n_z1 = n_z // 2
    span = n_y * tok
    quarter = tok // 4

    def rcopy(src, dst, recv, dev):
        return pltpu.make_async_remote_copy(
            src_ref=src, dst_ref=dst, send_sem=sent, recv_sem=recv,
            device_id=dev, device_id_type=MESH,
        )

    peers_a = []
    for dv in range(2):
        for dd in range(n_dp):
            if dv or dd:
                peers_a.append((v if dv == 0 else v_pair, lax.rem(d + dd, n_dp)))
    peers_b = [(2 * lax.rem(q + o, n_z) + p, d) for o in range(1, n_z)]
    barrier = pltpu.get_barrier_semaphore()
    for peer in peers_a + peers_b:
        pl.semaphore_signal(barrier, inc=1, device_id=peer, device_id_type=MESH)

    chunks = []
    for own, scr, tab, acc in ((th_own, th, table, tlog), (sh_own, sh, wgt, slog)):
        base = 0
        for width in chunk_widths(own.shape[1], tab is table):
            chunks.append((own, scr, tab, acc, base, width))
            base += width
    n_ch = len(chunks)
    firsts = [k == 0 or chunks[k][3] is not chunks[k - 1][3] for k in range(n_ch)]
    by_y = [False] * n_ch
    room = sum(ch[5] for ch in chunks) * 55 // 100
    for k in reversed(range(n_ch)):
        room -= chunks[k][5]
        if room < 0:
            break
        by_y[k] = True

    def block(g, yy):
        return pl.multiple_of((g * n_y + yy) * tok, tok)

    my_rows = pl.ds(pl.multiple_of((core * n_y + y) * tok, tok), tok)
    loads = []
    for k, (own, scr, tab, acc, base, width) in enumerate(chunks):
        src = codes if tab is table else weight
        cp = pltpu.make_async_copy(
            src.at[:, pl.ds(base, width)], tab.at[:, pl.ds(base, width)], ld_sem.at[k]
        )
        cp.start()
        loads.append(cp)
    own_loads = [
        pltpu.make_async_copy(th_own, th.at[my_rows], ld_sem.at[n_ch]),
        pltpu.make_async_copy(sh_own, sh.at[my_rows], ld_sem.at[n_ch + 1]),
    ]
    for cp in own_loads:
        cp.start()
    groups = scales.shape[0]
    pad = jnp.zeros((sc_rows.shape[1] - groups, LANE), jnp.float32)
    for b in range(0, scales.shape[1], LANE):
        sc_rows[pl.ds(b, LANE), :] = jnp.concatenate(
            [scales[:, pl.ds(b, LANE)], pad], axis=0
        ).T
    loss_row[...] = jnp.broadcast_to(
        loss_in[...].astype(jnp.float32).reshape(1, tok), loss_row.shape
    )
    lsc[core * n_y + y] = loss_row[...]
    with jax.named_scope("barrier"):
        pl.semaphore_wait(barrier, len(peers_a) + len(peers_b))

    A, B, C, E = 2 * r + p, 2 * r + 1 - p, 2 * (1 - r) + p, 2 * (1 - r) + 1 - p
    Y_A, X_A, Z_A, FAR, D_A, D_REST = range(6)
    order = []
    for i in range(n_z1):
        order += [i, n_z - 1 - i]
    order += [i for i in range(n_z) if i not in order]
    n_gw = sh.shape[1] // 512

    def run(c):
        mate = 2 * y + 1 - c
        X, Z = (v_pair, d), (v_quad, d)
        mate_slot = 0 if c == 1 else n_dp - 2
        sends = []

        def launch(cp):
            cp.start()
            sends.append(cp)

        def region(g, k, yy, piece, half=None):
            scr, base, width = chunks[k][1], chunks[k][4], chunks[k][5]
            first, size = block(g, yy) + piece * quarter, quarter
            if half is not None:
                size = quarter // 2
                first += half * size
            return scr.at[pl.ds(pl.multiple_of(first, size), size), pl.ds(base, width)]

        def came(o):
            return lax.rem(y + n_y - o, n_y)

        def y_send(k, kind):
            own, base, width = chunks[k][0], chunks[k][4], chunks[k][5]
            piece = A if kind == Y_A else E
            src = own.at[
                pl.ds(pl.multiple_of(piece * quarter, quarter), quarter), pl.ds(base, width)
            ]
            for o in range(1, n_y):
                to = 2 * lax.rem(y + o, n_y) + c
                launch(rcopy(src, region(c, k, y, piece), hop_r.at[kind, o - 1, k], (v, to)))

        def hop(kind, k, o, piece, dev, half=None):
            ref = region(c, k, came(o), piece, half)
            return rcopy(ref, ref, hop_r.at[kind, o - 1, k], dev)

        def to_mate(kind, k, o, piece):
            launch(hop(kind, k, o, piece, (v, mate)))

        def stage_y(k):
            for o in range(1, n_y):
                hop(Y_A, k, o, A, X).wait_recv()
                launch(hop(X_A, k, o, A, X))
                launch(hop(Z_A, k, o, A, Z))
                to_mate(D_A, k, o, A)

        def stage_xz(k):
            for o in range(1, n_y):
                hop(X_A, k, o, B, X).wait_recv()
                if not by_y[k]:
                    launch(hop(FAR, k, o, B, Z, 1))
                to_mate(D_REST, k, o, B)
                hop(Z_A, k, o, C, Z).wait_recv()
                if not by_y[k]:
                    launch(hop(FAR, k, o, C, X, 0))
                to_mate(D_REST, k, o, C)

        def stage_far(k):
            for o in range(1, n_y):
                hop(FAR, k, o, E, X).wait_recv()
                to_mate(D_REST, k, o, E)

        def mate_wait(kind, k):
            scr, base, width = chunks[k][1], chunks[k][4], chunks[k][5]
            size = quarter if kind == D_A else 3 * quarter
            for o in range(1, n_y):
                ref = scr.at[pl.ds(block(1 - c, came(o)), size), pl.ds(base, width)]
                rcopy(ref, ref, hop_r.at[kind, o - 1, k], X).wait_recv()

        def prepare(k, half):
            own, scr, tab, acc, base, width = chunks[k]
            if half == 0:
                loads[k].wait()
            steps = table.shape[0] // 128
            if tab is table:
                @pl.loop(half * steps, (half + 1) * steps)
                def _(i):
                    rsl = pl.ds(pl.multiple_of(i * 64, 64), 64)
                    sc = sc_rows[rsl, :]
                    for g in range(width // GROUP):
                        lane = pl.ds(base + g * GROUP, GROUP)
                        col = (base + g * GROUP) // GROUP
                        wide = table[rsl, lane].astype(jnp.float32) * sc[:, col : col + 1]
                        table[rsl, lane] = wide.astype(jnp.bfloat16)
            elif half == 0:
                for b in range(base, base + width, 256):
                    wgt_t[pl.ds(b, 256), :] = wgt[:, pl.ds(b, 256)].T

        def product(g, k):
            own, scr, tab, acc, base, width = chunks[k]
            for b in range(g * span, (g + 1) * span, 2 * tok):
                two = pl.ds(b, 2 * tok)
                half = tab.shape[0] // 2
                for h in range(2):
                    top = pl.ds(h * half, half)
                    part = dot_t(tab[top, pl.ds(base, width)], scr[two, pl.ds(base, width)])
                    if firsts[k]:
                        acc[top, two] = part
                    else:
                        acc[top, two] += part

        def local_stat(g):
            @pl.loop(0, n_y)
            def _(j):
                off = pl.multiple_of(j * tok, tok)
                sl = pl.ds(pl.multiple_of(g * span + j * tok, tok), tok)
                t_max = jnp.max(tlog[:, sl], axis=0, keepdims=True)
                s_max = jnp.max(slog[:, sl], axis=0, keepdims=True)
                te = jnp.exp(tlog[:, sl] - t_max)
                t_sum = jnp.sum(te, axis=0, keepdims=True)
                x_sum = jnp.sum(te * (tlog[:, sl] - slog[:, sl]), axis=0, keepdims=True)
                tlog[:, sl] = te
                se = jnp.exp(slog[:, sl] - s_max)
                s_sum = jnp.sum(se, axis=0, keepdims=True)
                slog[:, sl] = se
                stat[g, :, pl.ds(off, tok)] = jnp.concatenate(
                    [t_max, t_sum, x_sum, s_max, s_sum, jnp.zeros((3, tok), jnp.float32)],
                    axis=0,
                )

        def merge(parts):
            t_top = functools.reduce(jnp.maximum, [x[0:1] for x in parts])
            s_top = functools.reduce(jnp.maximum, [x[3:4] for x in parts])
            t_sum = x_sum = s_sum = 0.0
            for x in parts:
                t_w = jnp.exp(x[0:1] - t_top)
                t_sum += x[1:2] * t_w
                x_sum += x[2:3] * t_w
                s_sum += x[4:5] * jnp.exp(x[3:4] - s_top)
            return t_top, t_sum, x_sum, s_top, s_sum

        def a_copy(g, i):
            return rcopy(stat.at[g], in_a.at[g, i], a_r.at[g], peers_a[i])

        def b_copy(g, i):
            return rcopy(stat_b.at[g], in_b.at[g, i], b_r.at[g], peers_b[i])

        def exp_copies(g):
            sl = pl.ds(g * span, span)
            return [
                rcopy(tlog.at[:, sl], tl_m, e_r.at[0], (v, mate)),
                rcopy(slog.at[:, sl], sl_m, e_r.at[1], (v, mate)),
            ]

        def weight_copy():
            return rcopy(wgt_t, wgt_m, w_r, (v, mate))

        def send_a(g):
            local_stat(g)
            for i in reversed(range(len(peers_a))):
                launch(a_copy(g, i))
            if g != c:
                for cp in exp_copies(g):
                    launch(cp)

        def send_b(g):
            rcopy(in_a.at[g], in_a.at[g], a_r.at[g], X).wait_recv()
            stat_b[g] = jnp.concatenate(
                list(merge([stat[g]] + [in_a[g, i] for i in range(len(peers_a))]))
                + [jnp.zeros((3, span), jnp.float32)], axis=0
            )
            for i in range(len(peers_b)):
                launch(b_copy(g, i))

        def finish(g):
            rcopy(in_b.at[g], in_b.at[g], b_r.at[g], X).wait_recv()
            t_top, t_sum, x_sum, s_top, s_sum = merge(
                [stat_b[g]] + [in_b[g, i] for i in range(len(peers_b))]
            )
            t_lse = t_top + jnp.log(t_sum)
            s_lse = s_top + jnp.log(s_sum)
            fin[g] = jnp.concatenate(
                [
                    x_sum / t_sum - t_lse + s_lse,
                    jnp.exp(stat[g, 0:1] - t_lse),
                    jnp.exp(stat[g, 3:4] - s_lse),
                    jnp.exp(in_a[g, mate_slot, 0:1] - t_lse),
                    jnp.exp(in_a[g, mate_slot, 3:4] - s_lse),
                    jnp.zeros((3, span), jnp.float32),
                ],
                axis=0,
            )
            if g == c:
                kl_out[...] = fin[g, 0:1, pl.ds(pl.multiple_of(y * tok, tok), tok)]
                for cp in exp_copies(g):
                    cp.wait_recv()

            @pl.loop(0, n_y)
            def _(j):
                off = pl.multiple_of(j * tok, tok)
                sl = pl.ds(pl.multiple_of(g * span + j * tok, tok), tok)
                f = fin[g, :, pl.ds(off, tok)]
                grad[:, sl] = (
                    lsc[g * n_y + j][0:1] * (slog[:, sl] * f[2:3] - tlog[:, sl] * f[1:2])
                ).astype(jnp.bfloat16)
                if g == c:
                    at = pl.ds(off, tok)
                    grad_m[:, at] = (
                        lsc[g * n_y + j][0:1] * (sl_m[:, at] * f[4:5] - tl_m[:, at] * f[3:4])
                    ).astype(jnp.bfloat16)

        def hidden(z):
            for pp in range(2):
                at = pl.ds((2 * z + pp) * rv, rv)
                for yy in range(0, n_y, 2):
                    part = jnp.dot(
                        wgt_t[at, :], grad[:, pl.ds(c * span + yy * tok, 2 * tok)],
                        preferred_element_type=jnp.float32,
                    ) + jnp.dot(
                        wgt_m[at, :], grad_m[:, pl.ds(yy * tok, 2 * tok)],
                        preferred_element_type=jnp.float32,
                    )
                    for h in range(2):
                        mine[z, pp, yy + h] = part[:, h * tok : (h + 1) * tok]

        def y1_copy(z, o):
            to = 2 * lax.rem(y + o, n_y) + c
            return rcopy(y1s.at[z, o - 1], y1r.at[z, o - 1], r1r.at[z, o - 1], (v, to))

        def x1_copy(z):
            return rcopy(x1s.at[z], x1r.at[z], r2r.at[z, 0], (v_pair, d))

        def x2_copy(z):
            return rcopy(x2s.at[z - n_z1], x2r.at[z - n_z1], r1r.at[z, 0], (v_pair, d))

        def y2_copy(z, o):
            to = 2 * lax.rem(y + o, n_y) + c
            return rcopy(
                y2s.at[z - n_z1, o - 1], y2r.at[z - n_z1, o - 1], r2r.at[z, o - 1], (v, to),
            )

        def first_sends(z):
            if z < n_z1:
                for o in range(1, n_y):
                    to = lax.rem(y + o, n_y)
                    for pp in range(2):
                        y1s[z, o - 1, pp] = mine[z, pp, to].astype(jnp.bfloat16)
                    launch(y1_copy(z, o))
            else:
                for yy in range(n_y):
                    x2s[z - n_z1, yy] = mine[z, 1 - p, yy].astype(jnp.bfloat16)
                launch(x2_copy(z))

        def after_first(z):
            if z < n_z1:
                for o in range(1, n_y):
                    y1_copy(z, o).wait_recv()

                def total(which):
                    out = mine[z, which, y]
                    for o in range(1, n_y):
                        out += y1r[z, o - 1, which].astype(jnp.float32)
                    return out

                x1s[z] = total(1 - p).astype(jnp.bfloat16)
                launch(x1_copy(z))
                zf[z] = total(p)
            else:
                x2_copy(z).wait_recv()

                def total(yy):
                    return mine[z, p, yy] + x2r[z - n_z1, yy].astype(jnp.float32)

                for o in range(1, n_y):
                    y2s[z - n_z1, o - 1] = total(lax.rem(y + o, n_y)).astype(jnp.bfloat16)
                    launch(y2_copy(z, o))
                zf[z] = total(y)

        def z_copy(z):
            return rcopy(zs.at[z], zr.at[lax.rem(q + n_z - z, n_z) - 1], z_rs, (2 * z + p, d))

        def after_second(z):
            if z < n_z1:
                x1_copy(z).wait_recv()
                full = zf[z] + x1r[z].astype(jnp.float32)
            else:
                full = zf[z]
                for o in range(1, n_y):
                    y2_copy(z, o).wait_recv()
                    full += y2r[z - n_z1, o - 1].astype(jnp.float32)
            zf[z] = full
            zs[z] = full.astype(jnp.bfloat16)

            @pl.when(q != z)
            def _():
                z_copy(z).start()

        def weight_part(b):
            sl = pl.ds(b * 512, 512)
            gw_out[:, sl] = jnp.dot(
                grad[...], sh[:, sl], preferred_element_type=jnp.float32
            ).astype(jnp.bfloat16)

        def last():
            total = zf[q]
            rcopy(zr, zr, z_rs, X).wait_recv()
            for o in range(n_z - 1):
                total += zr[o].astype(jnp.float32)
            gh_out[...] = total.astype(jnp.bfloat16)

        def loss_wait():
            got = lsc.at[pl.ds(0, n_dp - 1)]
            rcopy(got, got, ls_r, X).wait_recv()

        def mate_copies():
            for i, (own, scr) in enumerate(((th_own, th), (sh_own, sh))):
                launch(rcopy(own, scr.at[pl.ds(block(c, y), tok)], pc_r.at[i], (v, mate)))

        def mate_arrived():
            for i, (own, scr) in enumerate(((th_own, th), (sh_own, sh))):
                rcopy(own, scr.at[pl.ds(block(1 - c, y), tok)], pc_r.at[i], (v, mate)).wait_recv()

        def named(name, fn, *args):
            with jax.named_scope(name + "_".join(str(x) for x in args if isinstance(x, int))):
                fn(*args)

        for dd in range(1, n_dp):
            launch(rcopy(loss_row, lsc.at[c * n_y + y], ls_r, (v, lax.rem(d + dd, n_dp))))
        far = [k for k in range(n_ch) if by_y[k]]

        def send_y(k):
            y_send(k, Y_A)
            if k == n_ch - 1:
                for kk in far:
                    y_send(kk, FAR)

        ops = {
            "p": lambda k: prepare(k, 0),
            "q": lambda k: prepare(k, 1),
            "s": send_y,
            "y": stage_y,
            "x": stage_xz,
            "f": stage_far,
            "d": lambda k: mate_wait(D_A, k),
            "m": lambda k: mate_wait(D_REST, k),
            "0": lambda k: product(0, k),
            "1": lambda k: product(1, k),
        }
        done = set()

        def play(steps, flush):
            todo = [(step[0], int(step[1:])) for step in steps]
            todo += [(name, k) for k in range(n_ch) for name in flush]
            for name, k in todo:
                if k < n_ch and (name, k) not in done:
                    done.add((name, k))
                    named(name, ops[name], k)

        if c == 0:
            play(("s0",), "")
            mate_copies()
            play(PLAY_A, "")
            for cp in own_loads:
                cp.wait()
            play(PLAY_B, "spqyxf0")
            named("send_a", send_a, 0)
            launch(weight_copy())
            named("mate_arrived", mate_arrived)
            play(PLAY_C, "")
            named("send_b", send_b, 0)
            play(PLAY_I, "dm1")
            named("send_a", send_a, 1)
            loss_wait()
            named("finish", finish, 0)
            weight_copy().wait_recv()
            for z in order:
                named("hidden", hidden, z)
                named("first_sends", first_sends, z)
            named("send_b", send_b, 1)
            for z in order:
                named("after_first", after_first, z)
            named("finish", finish, 1)
            for b in range(n_gw):
                named("weight", weight_part, b)
            for z in order:
                named("after_second", after_second, z)
            named("last", last)
        else:
            mate_copies()
            for k in range(n_ch):
                if chunks[k][2] is wgt:
                    play((f"p{k}",), "")
            launch(weight_copy())
            play(PLAY_D, "pq")
            for cp in own_loads:
                cp.wait()
            play(PLAY_E, "ds")
            named("mate_arrived", mate_arrived)
            play(PLAY_F, "m0")
            named("send_a", send_a, 0)
            play(PLAY_G, "")
            named("send_b", send_b, 0)
            play(PLAY_H, "yxf1")
            named("send_a", send_a, 1)
            loss_wait()
            named("finish", finish, 0)
            named("send_b", send_b, 1)
            weight_copy().wait_recv()
            named("finish", finish, 1)
            for z in order:
                named("hidden", hidden, z)
                named("first_sends", first_sends, z)
            for b in range(n_gw):
                named("weight", weight_part, b)
            for z in order:
                named("after_first", after_first, z)
            for z in order:
                named("after_second", after_second, z)
            named("last", last)

        for cp in sends:
            cp.wait_send()
        for o in range(1, n_z):
            z_copy(lax.rem(q + o, n_z)).wait_send()

    for which in range(2):
        pl.when(core == which)(functools.partial(run, which))


def hand_over(kl, gh, gw):
    parts = 4
    step = gw.shape[0] // parts

    def move(kl_in, gh_in, gw_in, kl_to, gh_to, gw_to, sem):
        plan = [(gh_in, gh_to), (kl_in, kl_to)]
        for i in range(parts):
            sl = pl.ds(i * step, step)
            plan.append((gw_in.at[sl], gw_to.at[sl]))
        writes = [pltpu.make_async_copy(a, b, sem.at[i]) for i, (a, b) in enumerate(plan)]
        for cp in writes:
            cp.start()
        for cp in writes:
            cp.wait()

    spec = pl.BlockSpec(memory_space=pl.ANY)
    arrays = (kl, gh, gw)
    return pl.pallas_call(
        move,
        out_shape=tuple(jax.ShapeDtypeStruct(a.shape, a.dtype) for a in arrays),
        in_specs=[pl.BlockSpec(memory_space=pltpu.VMEM)] * 3,
        out_specs=(spec,) * 3,
        scratch_shapes=[pltpu.SemaphoreType.DMA((parts + 2,))],
        compiler_params=pltpu.CompilerParams(vmem_limit_bytes=4 * 1024 * 1024),
        name="hand_over",
    )(*arrays)


def solution(mesh):
    n_vocab, n_dp = mesh.shape["vocab"], mesh.shape["dp"]

    def local(th_own, sh_own, codes, scales, weight, loss_scale):
        tok, dt = th_own.shape
        ds_ = sh_own.shape[1]
        rows = codes.shape[0]
        n_tok = tok * n_dp
        n_y, n_z = n_dp // 2, n_vocab // 2
        n_off, n_z1 = n_y - 1, n_z // 2
        n_z2 = n_z - n_z1
        rv = ds_ // n_vocab
        n_ch = len(chunk_widths(dt, True)) + len(chunk_widths(ds_, False))
        span = n_y * tok
        n_a, n_b = 2 * n_dp - 1, n_z - 1
        bf, f32 = jnp.bfloat16, jnp.float32
        V, D = pltpu.VMEM, pltpu.SemaphoreType.DMA
        any_spec = pl.BlockSpec(memory_space=pl.ANY)
        vm_spec = pl.BlockSpec(memory_space=pltpu.VMEM)
        kl, gh, gw = pl.pallas_call(
            functools.partial(kernel, n_vocab, n_dp),
            out_shape=(
                pltpu.VMEM((1, tok), f32),
                pltpu.VMEM((rv, tok), bf),
                pltpu.VMEM((rows, ds_), bf),
            ),
            in_specs=[any_spec, any_spec, any_spec, vm_spec, any_spec, vm_spec],
            out_specs=(vm_spec, vm_spec, vm_spec),
            scratch_shapes=[
                V((n_tok, dt), bf), V((n_tok, ds_), bf), V((rows, dt), bf), V((rows, ds_), bf),
                V((ds_, rows), bf), V((rows, n_tok), f32), V((rows, n_tok), f32),
                V((n_dp, 8, tok), f32), V((2, 8, span), f32), V((2, 8, span), f32),
                V((2, 8, span), f32), V((2, n_a, 8, span), f32), V((2, n_b, 8, span), f32),
                V((rows, n_tok), bf),
                V((rows, span), bf), V((ds_, rows), bf), V((rows, span), f32),
                V((rows, span), f32), V((n_z, 2, n_y, rv, tok), f32),
                V((n_z1, n_off, 2, rv, tok), bf), V((n_z1, n_off, 2, rv, tok), bf),
                V((n_z1, rv, tok), bf), V((n_z1, rv, tok), bf),
                V((n_z2, n_y, rv, tok), bf), V((n_z2, n_y, rv, tok), bf),
                V((n_z2, n_off, rv, tok), bf), V((n_z2, n_off, rv, tok), bf),
                V((n_z, rv, tok), bf), V((n_z - 1, rv, tok), bf), V((n_z, rv, tok), f32),
                V((rows, -(-scales.shape[1] // 8) * 8), f32), V((8, tok), f32),
                D((n_ch + 2,)), D((2,)), D((6, n_off, n_ch)), D, D, D((2,)), D((2,)),
                D, D((2,)), D((n_z, n_off)), D((n_z, n_off)), D,
            ],
            compiler_params=pltpu.CompilerParams(
                collective_id=0, has_side_effects=True, vmem_limit_bytes=56 * 1024 * 1024
            ),
            name="distill",
        )(th_own, sh_own, codes, scales.T, weight, loss_scale)
        kl, gh, gw = hand_over(kl, gh, gw)
        return kl.reshape(tok), gh.T, gw

    in_specs = (
        P("dp", None),
        P("dp", None),
        P(("vocab", "dp"), None),
        P(("vocab", "dp"), None),
        P(("vocab", "dp"), None),
        P("dp"),
    )
    out_specs = (P("dp"), P("dp", "vocab"), P(("vocab", "dp"), None))
    return jax.shard_map(local, mesh=mesh, in_specs=in_specs, out_specs=out_specs, check_vma=False)
```
